32 devices in a mesh: blk: 16 (over z, y, core), uly: 2 (over x).
Axes of the slice: x: 2, y: 2, z: 4, core: 2. Of those that a mesh axis runs over, the one named last changes fastest.
Arguments:
- query_rows: bfloat16 [4096, 8192], P(('blk', 'uly')), may hold values from -6 to 6
- key_rows: bfloat16 [4096, 1024], P(('blk', 'uly')), may hold values from -6 to 6
- value_rows: bfloat16 [4096, 1024], P(('blk', 'uly')), may hold values from -6 to 6
- out_grad: bfloat16 [4096, 8192], P(('blk', 'uly')), may hold values from -6 to 6
- segment_ids: int32 [4096], P(('blk', 'uly')), may hold values from 0 to 15, never falling along the last dimension, each value on 1 to 1024 neighbouring positions
Outputs:
- attn_out: bfloat16 [4096, 8192], P(('blk', 'uly'))
- query_grad: bfloat16 [4096, 8192], P(('blk', 'uly'))
- key_grad: bfloat16 [4096, 1024], P(('blk', 'uly'))
- value_grad: bfloat16 [4096, 1024], P(('blk', 'uly'))
The draws below stay inside these ranges and needn't reach their ends.
Inputs may be any that keep to these rules, and one draw needn't show every extreme that they name: `segment_ids`: segment numbers never fall along the sequence and start at 0; each segment holds 1 to 1024 positions, and one holds exactly that many.
All inputs are finite; a program needn't handle non-finite values.
Results may differ from the reference program's by a relative error of at most 0.0096.
Values may be sent and summed in bfloat16 or wider, within the bound.
No kernel may reach another device: no remote copies, remote signals or barrier semaphores. Data moves between devices by JAX's collectives and lax.ppermute only.
A program may use at most 128 MiB of HBM per device.

```python
import math
import jax
import jax.numpy as jnp
import numpy as np
from jax import lax

Q_HEADS = 64
KV_HEADS = 8
HEAD_DIM = 128
ROWS_DEV = 256
GROUP_SIZE = 8
LENGTH = 4096
N_BLK = 16


def draw_query_rows(key, part):
    field_key = jax.random.fold_in(key, 1)
    shape_full = (LENGTH, Q_HEADS * HEAD_DIM)
    field = jnp.clip(3.0 * jax.random.normal(field_key, shape_full, jnp.float32), -6.0, 6.0)
    return field.astype(jnp.bfloat16)


def draw_key_rows(key, part):
    field_key = jax.random.fold_in(key, 2)
    shape_full = (LENGTH, KV_HEADS * HEAD_DIM)
    field = jnp.clip(0.5 * jax.random.normal(field_key, shape_full, jnp.float32), -2.5, 2.5)
    return field.astype(jnp.bfloat16)


def steps_of(stream_key, extent, shards, smallest, largest):
    gain = 1.0
    for axis_at, blocks in shards:
        steps = jax.random.uniform(jax.random.fold_in(jax.random.fold_in(stream_key, 6), axis_at), (blocks,), jnp.float32, smallest / len(shards), largest / len(shards))
        gain = gain * jnp.repeat(jnp.exp(steps), extent[axis_at] // blocks).reshape((-1,) + (1,) * (len(extent) - 1 - axis_at))
    return gain


def length_profile(number_of, total, limit, skew):
    weights = [(1 << 20) // math.isqrt(standing ** skew) + 1 for standing in range(2, number_of + 1)]
    surplus, holding = total - limit - (number_of - 1), [1] * (number_of - 1)
    while surplus > 0:
        candidates = [i for i in range(number_of - 1) if holding[i] < limit]
        whole, budget = sum([weights[i] for i in candidates]), surplus
        for i in candidates:
            addition = min(limit - holding[i], max(1, budget * weights[i] // whole), surplus)
            holding[i] = holding[i] + addition
            surplus = surplus - addition
    return np.array([limit] + holding)


def uneven_parts(rng, number_of, total, reach, skew):
    if number_of == 2:
        one = jax.random.randint(rng, (), max(1, total - reach), min(reach, total - 1) + 1)
        return jnp.stack([one, total - one])
    tallies = jnp.asarray(length_profile(number_of, total, reach, skew), jnp.int32)
    twos = (number_of - 1) // 2
    source_of, taker = tallies[1:1 + 2 * twos:2], tallies[2:2 + 2 * twos:2]
    room = jnp.minimum(source_of - 1, reach - taker)
    passed = jax.random.randint(jax.random.fold_in(rng, 1), (twos,), 0, 1 << 20) % (room + 1)
    tallies = tallies.at[1:1 + 2 * twos:2].set(source_of - passed).at[2:2 + 2 * twos:2].set(taker + passed)
    return tallies[jax.random.permutation(jax.random.fold_in(rng, 2), number_of)]


def normal_values(rng, extent, scale, bound, shards=(), kind=jnp.bfloat16):
    entries = scale * jax.random.normal(rng, extent, jnp.float32)
    if shards:
        entries = entries * steps_of(rng, extent, shards, -0.22, 0.18)
    return jnp.clip(entries, -bound, bound).astype(kind)


def setup_inputs(seed: int = 0) -> dict:
    key_of = jax.random.split(jax.random.key(seed), 6)
    return {
        "query_rows": draw_query_rows(jax.random.fold_in(key_of[5], 71), 0),
        "key_rows": draw_key_rows(jax.random.fold_in(key_of[5], 71), 0),
        "value_rows": normal_values(key_of[2], (LENGTH, KV_HEADS * HEAD_DIM), 1.0, 6.0, ((0, 32),)),
        "out_grad": normal_values(key_of[3], (LENGTH, Q_HEADS * HEAD_DIM), 1.0, 6.0, ((0, 32),)),
        "segment_ids": jnp.searchsorted(jnp.cumsum(uneven_parts(key_of[4], N_BLK, LENGTH, 4 * ROWS_DEV, 1)), jnp.arange(LENGTH), side="right").astype(jnp.int32),
    }


masked_score = -1e+30

def reference(query_rows, key_rows, value_rows, out_grad, segment_ids):
    seq_length = query_rows.shape[0]
    score_scale = 1.0 / math.sqrt(HEAD_DIM)
    query_span = math.gcd(seq_length, 512)
    block_count = seq_length // query_span
    prompt_rows = 4 * ROWS_DEV
    band_len = min(prompt_rows + query_span, seq_length)
    prompt_pos = jnp.arange(prompt_rows, dtype=jnp.int32)
    band_steps = jnp.arange(band_len, dtype=jnp.int32)
    query_heads = query_rows.reshape(seq_length, KV_HEADS, GROUP_SIZE, HEAD_DIM).transpose(1, 0, 2, 3)
    grad_heads = out_grad.reshape(seq_length, KV_HEADS, GROUP_SIZE, HEAD_DIM).transpose(1, 0, 2, 3)
    key_heads = key_rows.reshape(seq_length, KV_HEADS, HEAD_DIM).transpose(1, 0, 2)
    value_heads = value_rows.reshape(seq_length, KV_HEADS, HEAD_DIM).transpose(1, 0, 2)

    def one_head(operands):
        query_group, grad_group, key_group, value_group = operands
        key_wide = key_group.astype(jnp.float32)
        value_wide = value_group.astype(jnp.float32)

        def one_block(totals, block_index):
            key_acc, value_acc = totals
            row_first = (block_index * query_span).astype(jnp.int32)
            band_first = jnp.clip(row_first - prompt_rows, 0, seq_length - band_len).astype(jnp.int32)
            key_pos = jnp.concatenate([prompt_pos, band_first + band_steps])
            key_segs = jnp.concatenate([segment_ids[:prompt_rows], lax.dynamic_slice_in_dim(segment_ids, band_first, band_len)])
            keep = jnp.concatenate([prompt_pos >= 0, band_first + band_steps >= prompt_rows])
            keys = jnp.concatenate([key_wide[:prompt_rows], lax.dynamic_slice_in_dim(key_wide, band_first, band_len)])
            values = jnp.concatenate([value_wide[:prompt_rows], lax.dynamic_slice_in_dim(value_wide, band_first, band_len)])
            query_block = lax.dynamic_slice_in_dim(query_group, row_first, query_span).astype(jnp.float32)
            grad_block = lax.dynamic_slice_in_dim(grad_group, row_first, query_span).astype(jnp.float32)
            query_pos = row_first + jnp.arange(query_span, dtype=jnp.int32)
            query_segs = lax.dynamic_slice_in_dim(segment_ids, row_first, query_span)
            causal = key_pos[None, :] <= query_pos[:, None]
            shared = (key_segs[None, :] == query_segs[:, None]) | (key_segs[None, :] == 0)
            visible_map = (causal & shared & keep[None, :])[None]
            scores = jnp.einsum('qpd,kd->pqk', query_block, keys) * score_scale
            scores = jnp.where(visible_map, scores, masked_score)
            row_peak = lax.optimization_barrier(jnp.max(scores, axis=-1, keepdims=True))
            row_mass = lax.optimization_barrier(jnp.sum(jnp.where(visible_map, jnp.exp(scores - row_peak), 0.0), axis=-1, keepdims=True))
            log_norm = row_peak + jnp.log(row_mass)
            weights = jnp.where(visible_map, jnp.exp(scores - log_norm), 0.0)
            weights_low = lax.optimization_barrier(weights.astype(jnp.bfloat16)).astype(jnp.float32)
            attn_block = jnp.einsum('pqk,kd->qpd', weights_low, values).astype(jnp.bfloat16)
            grad_dots = jnp.einsum('qpd,kd->pqk', grad_block, values)
            delta = lax.optimization_barrier(jnp.sum(weights * grad_dots, axis=-1, keepdims=True))
            slopes = lax.optimization_barrier((weights * (grad_dots - delta)).astype(jnp.bfloat16)).astype(jnp.float32)
            query_part = (jnp.einsum('pqk,kd->qpd', slopes, keys) * score_scale).astype(jnp.bfloat16)
            key_terms = jnp.einsum('pqk,qpd->kd', slopes, query_block)
            value_terms = jnp.einsum('pqk,qpd->kd', weights_low, grad_block)
            key_acc = key_acc.at[:prompt_rows].add(key_terms[:prompt_rows])
            value_acc = value_acc.at[:prompt_rows].add(value_terms[:prompt_rows])
            key_band = lax.dynamic_slice_in_dim(key_acc, band_first, band_len) + key_terms[prompt_rows:]
            value_band = lax.dynamic_slice_in_dim(value_acc, band_first, band_len) + value_terms[prompt_rows:]
            zero_index = jnp.zeros((), jnp.int32)
            key_acc = lax.dynamic_update_slice(key_acc, key_band, (band_first, zero_index))
            value_acc = lax.dynamic_update_slice(value_acc, value_band, (band_first, zero_index))
            return ((key_acc, value_acc), (attn_block, query_part))
        zeroes = jnp.zeros((seq_length, HEAD_DIM), jnp.float32)
        totals, blocks = lax.scan(one_block, (zeroes, zeroes), jnp.arange(block_count, dtype=jnp.int32))
        attn_group = blocks[0].reshape(seq_length, GROUP_SIZE, HEAD_DIM)
        query_group_grad = blocks[1].reshape(seq_length, GROUP_SIZE, HEAD_DIM)
        key_group_grad = (totals[0] * score_scale).astype(jnp.bfloat16)
        value_group_grad = totals[1].astype(jnp.bfloat16)
        return (attn_group, query_group_grad, key_group_grad, value_group_grad)
    attn_all, query_all, key_all, value_all = lax.map(one_head, (query_heads, grad_heads, key_heads, value_heads))
    attn_out = attn_all.transpose(1, 0, 2, 3).reshape(seq_length, Q_HEADS * HEAD_DIM)
    query_grad = query_all.transpose(1, 0, 2, 3).reshape(seq_length, Q_HEADS * HEAD_DIM)
    key_grad = key_all.transpose(1, 0, 2).reshape(seq_length, KV_HEADS * HEAD_DIM)
    value_grad = value_all.transpose(1, 0, 2).reshape(seq_length, KV_HEADS * HEAD_DIM)
    return (attn_out, query_grad, key_grad, value_grad)
```

```python
import functools
import math

import jax
import jax.numpy as jnp
import numpy as np
from jax import lax
from jax.experimental import pallas as pl
from jax.experimental.pallas import tpu as pltpu
from jax.sharding import Mesh
from jax.sharding import PartitionSpec as P

HEAD_DIM = 128
BLOCK = 256
LIMIT = 1024
NEG = -1e30
FAR = 1 << 30
ALL = ("z", "y", "c", "x")
CORES = 2
F32 = jnp.float32
BF16 = jnp.bfloat16


def dot(a, b, dims):
    return lax.dot_general(a, b, (dims, ((), ())), preferred_element_type=F32)


def attention_kernel(n_sub, chunk, group, parts, *refs):
    need, kinfo, rinfo = refs[:3]
    q_refs, g_refs = refs[3:5], refs[5:7]
    at = 7
    kv_refs = []
    for _ in parts:
        kv_refs.append(refs[at : at + n_sub])
        at += n_sub
    o_refs, dq_refs = refs[at : at + 2], refs[at + 2 : at + 4]
    at += 4
    dkv_refs = []
    for _ in parts:
        dkv_refs.append(refs[at : at + n_sub])
        at += n_sub
    kv, dkv, bias, s_buf, dp_buf, m_buf, l_buf, d_buf, acc, q_all, g_all = refs[at:]
    n_blocks = sum(parts)
    rows = group * chunk
    scale = 1.0 / math.sqrt(HEAD_DIM)
    log_scale = scale * math.log2(math.e)
    d = HEAD_DIM

    base = 0
    for s, n in enumerate(parts):
        for b in range(n):
            for k in range(n_sub):
                kv[base + b, pl.ds(k * chunk, chunk), :] = kv_refs[s][k][b]
        base += n
    dkv[...] = jnp.zeros_like(dkv)

    @pl.when(pl.program_id(0) == 0)
    def _():
        for r in range(CORES):
            rpos = rinfo[r, 0]
            rseg = rinfo[r, 1]
            for b in range(n_blocks):
                kpos = kinfo[b, 0:1, :]
                kseg = kinfo[b, 1:2, :]
                seen = (kpos <= rpos) & ((kseg == rseg) | (kseg == 0))
                bias[r, b] = jnp.where(seen, 0.0, NEG)

    for r in range(CORES):
        for h in range(group):
            q_all[pl.ds(h * chunk, chunk), :] = q_refs[r][:, h * d : (h + 1) * d]
            g_all[pl.ds(h * chunk, chunk), :] = g_refs[r][:, h * d : (h + 1) * d]
        m_buf[...] = jnp.full_like(m_buf, NEG)

        def each(fn):
            def turn(b, carry):
                @pl.when(need[r * n_blocks + b] > 0)
                def _():
                    fn(b)

                return carry

            lax.fori_loop(0, n_blocks, turn, 0)

        def score_pass(b):
            s = dot(q_all[...], kv[b, :, :d], ((1,), (1,))) * log_scale
            s = (s.reshape(group, chunk, BLOCK) + bias[r, b][None]).reshape(rows, BLOCK)
            s_buf[b] = s
            m_buf[...] = jnp.maximum(m_buf[...], jnp.maximum(s[:, :d], s[:, d:]))

        each(score_pass)
        m_buf[...] = jnp.broadcast_to(jnp.max(m_buf[...], axis=1, keepdims=True), m_buf.shape)
        l_buf[...] = jnp.zeros_like(l_buf)
        d_buf[...] = jnp.zeros_like(d_buf)
        acc[...] = jnp.zeros_like(acc)

        def weight_pass(b):
            m = m_buf[...]
            p = jnp.exp2(s_buf[b] - jnp.concatenate([m, m], axis=1))
            dp = dot(g_all[...], kv[b, :, d:], ((1,), (1,)))
            s_buf[b] = p
            dp_buf[b] = dp
            l_buf[...] += p[:, :d] + p[:, d:]
            pd = p * dp
            d_buf[...] += pd[:, :d] + pd[:, d:]
            acc[...] += dot(p.astype(BF16), kv[b, :, d:], ((1,), (0,)))

        each(weight_pass)
        inv = 1.0 / jnp.sum(l_buf[...], axis=1, keepdims=True)
        delta = jnp.sum(d_buf[...], axis=1, keepdims=True) * inv
        l_buf[...] = jnp.broadcast_to(inv, l_buf.shape)
        d_buf[...] = jnp.broadcast_to(delta, d_buf.shape)
        out = (acc[...] * inv).astype(BF16)
        for h in range(group):
            o_refs[r][:, h * d : (h + 1) * d] = out[h * chunk : (h + 1) * chunk]
        acc[...] = jnp.zeros_like(acc)

        def slope_pass(b):
            inv = l_buf[...]
            delta = d_buf[...]
            w = s_buf[b] * jnp.concatenate([inv, inv], axis=1)
            ds = (w * (dp_buf[b] - jnp.concatenate([delta, delta], axis=1))).astype(BF16)
            acc[...] += dot(ds, kv[b, :, :d], ((1,), (0,)))
            dkv[b, :, :d] += dot(ds, q_all[...], ((0,), (0,)))
            dkv[b, :, d:] += dot(w.astype(BF16), g_all[...], ((0,), (0,)))

        each(slope_pass)
        out = (acc[...] * scale).astype(BF16)
        for h in range(group):
            dq_refs[r][:, h * d : (h + 1) * d] = out[h * chunk : (h + 1) * chunk]

    base = 0
    for s, n in enumerate(parts):
        for b in range(n):
            for k in range(n_sub):
                rows_k = pl.ds(k * chunk, chunk)
                dkv_refs[s][k][b, :, :d] = (dkv[base + b, rows_k, :d] * scale).astype(BF16)
                dkv_refs[s][k][b, :, d:] = dkv[base + b, rows_k, d:].astype(BF16)
        base += n


def attention(need, kinfo, rinfo, q_pair, g_pair, kv_sets, group):
    chunk = q_pair[0].shape[0]
    n_sub = len(kv_sets[0])
    heads = q_pair[0].shape[1] // (group * HEAD_DIM)
    parts = tuple(s[0].shape[0] for s in kv_sets)
    n_blocks = sum(parts)
    rows = group * chunk
    width = group * HEAD_DIM
    pair = 2 * HEAD_DIM
    whole = lambda shape: pl.BlockSpec(shape, lambda h: (0,) * len(shape))
    row_spec = pl.BlockSpec((chunk, width), lambda h: (0, h))
    kv_specs = [
        pl.BlockSpec((n, chunk, pair), lambda h: (0, 0, h)) for n in parts for _ in range(n_sub)
    ]
    row_out = jax.ShapeDtypeStruct(q_pair[0].shape, BF16)
    pairs = rows * n_blocks * BLOCK * CORES * heads
    outs = pl.pallas_call(
        functools.partial(attention_kernel, n_sub, chunk, group, parts),
        grid=(heads,),
        in_specs=[pl.BlockSpec(memory_space=pltpu.SMEM), whole(kinfo.shape), whole(rinfo.shape)]
        + [row_spec] * 4
        + kv_specs,
        out_specs=[row_spec] * 4 + kv_specs,
        out_shape=[row_out] * 4
        + [jax.ShapeDtypeStruct(a.shape, BF16) for s in kv_sets for a in s],
        scratch_shapes=[
            pltpu.VMEM((n_blocks, BLOCK, pair), BF16),
            pltpu.VMEM((n_blocks, BLOCK, pair), F32),
            pltpu.VMEM((CORES, n_blocks, chunk, BLOCK), F32),
            pltpu.VMEM((n_blocks, rows, BLOCK), F32),
            pltpu.VMEM((n_blocks, rows, BLOCK), F32),
            pltpu.VMEM((rows, HEAD_DIM), F32),
            pltpu.VMEM((rows, HEAD_DIM), F32),
            pltpu.VMEM((rows, HEAD_DIM), F32),
            pltpu.VMEM((rows, HEAD_DIM), F32),
            pltpu.VMEM((rows, HEAD_DIM), BF16),
            pltpu.VMEM((rows, HEAD_DIM), BF16),
        ],
        compiler_params=pltpu.CompilerParams(vmem_limit_bytes=56 << 20),
        cost_estimate=pl.CostEstimate(
            flops=4 * pairs * HEAD_DIM, bytes_accessed=16 << 20, transcendentals=pairs
        ),
        name="attention",
    )(need, kinfo, rinfo, *q_pair, *g_pair, *[a for s in kv_sets for a in s])
    o_pair, dq_pair = outs[:2], outs[2:4]
    grads = [
        outs[4 + i * n_sub : 4 + (i + 1) * n_sub] for i in range(len(parts))
    ]
    return o_pair, dq_pair, grads


def per_device(query_rows, key_rows, value_rows, out_grad, segment_ids):
    chunk = query_rows.shape[0]
    planes, n_sub = lax.axis_size("z"), lax.axis_size("x")
    halves = 2 * planes
    z, y, c, x = (lax.axis_index(a) for a in ALL)
    half = 2 * z + y
    devices = planes * 2 * CORES * n_sub
    kv_heads = key_rows.shape[1] // HEAD_DIM
    group = query_rows.shape[1] // key_rows.shape[1]
    my_heads = kv_heads // CORES
    pair = 2 * HEAD_DIM

    def swap_cores(a):
        return lax.ppermute(a, "c", [(0, 1), (1, 0)])

    def rotate(a, by):
        return lax.ppermute(a, "x", [(i, (i + by) % n_sub) for i in range(n_sub)])

    def shift(a, by):
        moves = [(i, i + by) for i in range(halves) if 0 <= i + by < halves]
        return lax.ppermute(a, ("z", "y"), moves)

    def spread(a):
        return [a] + [rotate(a, k) for k in range(1, n_sub)]

    def gather_back(arrays):
        total = arrays[0].astype(F32)
        for k in range(1, n_sub):
            total = total + rotate(arrays[k], -k).astype(F32)
        return total

    ids = lax.all_to_all(
        jnp.broadcast_to(segment_ids[None], (devices, chunk)), ALL, split_axis=0, concat_axis=0, tiled=True
    )

    kv = jnp.concatenate(
        [key_rows.reshape(chunk, kv_heads, HEAD_DIM), value_rows.reshape(chunk, kv_heads, HEAD_DIM)], axis=2
    ).reshape(chunk, CORES, my_heads * pair)
    take = lambda a, i: lax.dynamic_index_in_dim(a, i, 1, keepdims=False)
    kv_mine = jnp.stack([take(kv, c), swap_cores(take(kv, 1 - c))])
    q_cols = query_rows.reshape(chunk, CORES, -1)
    g_cols = out_grad.reshape(chunk, CORES, -1)
    q_pair = (take(q_cols, c), swap_cores(take(q_cols, 1 - c)))
    g_pair = (take(g_cols, c), swap_cores(take(g_cols, 1 - c)))

    own_set = spread(kv_mine)
    set_1 = spread(shift(kv_mine, 1))
    set_2 = spread(shift(kv_mine, 2))

    n0 = jnp.sum((ids == 0).astype(jnp.int32))
    row_chunk = [(2 * half + (c ^ r)) * n_sub + x for r in range(CORES)]
    row_pos = jnp.stack([i * chunk + jnp.arange(chunk, dtype=jnp.int32) for i in row_chunk])
    row_seg = jnp.stack([lax.dynamic_index_in_dim(ids, i, 0, keepdims=False) for i in row_chunk])
    rinfo = jnp.stack([row_pos, row_seg], axis=1)[..., None]
    starts = jnp.sum((ids[None] < row_seg[:, :1, None]).astype(jnp.int32), axis=(1, 2))
    sub = (x - jnp.arange(n_sub, dtype=jnp.int32)) % n_sub

    def branch(prompt_blocks):
        def run(_):
            wide = prompt_blocks > 1
            prompt = kv_mine if wide else lax.dynamic_index_in_dim(kv_mine, c, 0)
            step = planes // 2
            while step:
                got = lax.ppermute(prompt, "z", [(i, i + step) for i in range(0, planes, 2 * step)])
                prompt = jnp.where(z % (2 * step) == step, got, prompt)
                step //= 2
            if wide:
                other = lax.ppermute(prompt, "y", [(0, 1), (1, 0)])
                prompt = jnp.concatenate(
                    [jnp.where(y == 0, prompt, other), jnp.where(y == 0, other, prompt)]
                )
                prompt_index = jnp.stack([c, 1 - c, 2 + c, 3 - c])
            else:
                prompt = jnp.where(y == 0, prompt, lax.ppermute(prompt, "y", [(0, 1)]))
                prompt_index = jnp.zeros((1,), jnp.int32)
            prompt_set = spread(prompt)

            band = jnp.stack([2 * (half - s) + (c ^ k) for s in range(3) for k in range(CORES)])
            block = jnp.concatenate([band, prompt_index])
            usable = jnp.concatenate([band >= prompt_blocks, jnp.full(prompt_index.shape, True)])
            key_chunk = jnp.clip(block, 0)[:, None] * n_sub + sub[None]
            key_seg = jnp.take(ids, key_chunk.reshape(-1), axis=0).reshape(-1, BLOCK)
            key_pos = (
                key_chunk[..., None] * chunk + jnp.arange(chunk, dtype=jnp.int32)
            ).reshape(-1, BLOCK)
            key_pos = jnp.where(usable[:, None], key_pos, FAR)
            kinfo = jnp.stack([key_pos, key_seg], axis=1)
            first = block * BLOCK
            need = (
                usable[None]
                & (first[None] <= row_pos[:, -1:])
                & ((first[None] < n0) | (first[None] + BLOCK > starts[:, None]))
            )
            need = need.astype(jnp.int32).reshape(-1)

            o_pair, dq_pair, grads = attention(
                need, kinfo, rinfo, q_pair, g_pair, [own_set, set_1, set_2, prompt_set], group
            )

            total = gather_back(grads[0])
            total = total + shift(gather_back(grads[1]).astype(BF16), -1).astype(F32)
            total = total + shift(gather_back(grads[2]).astype(BF16), -2).astype(F32)
            back = gather_back(grads[3]).astype(BF16)
            if wide:
                keep = jnp.where(y == 0, back[:2], back[2:])
                send = jnp.where(y == 0, back[2:], back[:2])
                got = lax.ppermute(send, "y", [(0, 1), (1, 0)])
                back = keep.astype(F32) + got.astype(F32)
            else:
                back = back.astype(F32) + lax.ppermute(back, "y", [(1, 0)]).astype(F32)
            step = 1
            while step < planes:
                got = lax.ppermute(
                    back.astype(BF16), "z", [(i + step, i) for i in range(0, planes, 2 * step)]
                )
                back = back + got.astype(F32)
                step *= 2
            here = (z == 0) if wide else (z == 0) & (y == 0)
            back = jnp.where(here, back, 0.0)
            if wide:
                total = total + back
            else:
                place = (jnp.arange(CORES) == c)[:, None, None]
                total = total + jnp.where(place, back, 0.0)
            total = total.astype(BF16)
            return o_pair[0], o_pair[1], dq_pair[0], dq_pair[1], total

        return run

    o_mine, o_other, dq_mine, dq_other, grads = lax.cond(
        n0 <= BLOCK, branch(1), branch(LIMIT // BLOCK), 0
    )

    def join(mine, other):
        got = swap_cores(other)
        low = jnp.where(c == 0, mine, got)
        high = jnp.where(c == 0, got, mine)
        return jnp.concatenate([low, high], axis=1)

    kv_grad = join(grads[0], grads[1]).reshape(chunk, kv_heads, 2, HEAD_DIM)
    key_grad = kv_grad[:, :, 0].reshape(chunk, -1)
    value_grad = kv_grad[:, :, 1].reshape(chunk, -1)
    return join(o_mine, o_other), join(dq_mine, dq_other), key_grad, value_grad


def solution(mesh):
    blk, uly = mesh.shape["blk"], mesh.shape["uly"]
    parts = Mesh(np.asarray(mesh.devices).reshape(blk // 4, 2, CORES, uly), ALL)
    rows = P(ALL, None)
    return jax.shard_map(
        per_device,
        mesh=parts,
        in_specs=(rows, rows, rows, rows, P(ALL)),
        out_specs=(rows, rows, rows, rows),
        check_vma=False,
    )
```

```python
import functools
import math

import jax
import jax.numpy as jnp
import numpy as np
from jax import lax
from jax.experimental import pallas as pl
from jax.experimental.pallas import tpu as pltpu
from jax.sharding import Mesh
from jax.sharding import PartitionSpec as P

HEAD_DIM = 128
BLOCK = 256
WIDE = 4
NEG = -1e30
FAR = 1 << 30
ALL = ("z", "y", "c", "x")
CORES = 2
SPLIT = 2
F32 = jnp.float32
BF16 = jnp.bfloat16


def dot(a, b, dims):
    return lax.dot_general(a, b, (dims, ((), ())), preferred_element_type=F32)


def attention_kernel(n_sub, chunk, group, first_call, wide_column, parts, *refs):
    info, kinfo, rinfo = refs[:3]
    q_refs, g_refs = refs[3:5], refs[5:7]
    at = 7
    kv_refs = []
    for _ in parts:
        kv_refs.append(refs[at : at + n_sub])
        at += n_sub
    if not first_call:
        at += 4
    o_refs, dq_refs = refs[at : at + 2], refs[at + 2 : at + 4]
    at += 4
    dkv_refs = []
    for _ in parts:
        dkv_refs.append(refs[at : at + n_sub])
        at += n_sub
    order, kv, dkv, bias, s_buf, dp_buf, m_buf, l_buf, d_buf, acc, q_all, g_all, o_all, dq_all = refs[at:]
    n_blocks = parts[-1][0] + parts[-1][1]
    rows = group * chunk
    scale = 1.0 / math.sqrt(HEAD_DIM)
    log_scale = scale * math.log2(math.e)
    d = HEAD_DIM
    wide = info[1] > 0

    def load(s):
        base, n = parts[s]
        for b in range(n):
            for k in range(n_sub):
                kv[base + b, pl.ds(k * chunk, chunk), :] = kv_refs[s][k][b]

    for s in range(len(parts) - 1):
        load(s)
    plain = parts[-1][0]
    head = pl.program_id(0)
    pair = 2 * d

    def wide_part(array, k, column):
        here = kv.at[pl.ds(plain, n_blocks - plain), pl.ds(k * chunk, chunk), :]
        return here, array.at[:, :, pl.ds(pl.multiple_of(column * pair, pair), pair)]

    @pl.when(wide)
    def _():
        for k in range(n_sub):
            here, there = wide_part(kv_refs[-1][k], k, wide_column + head)
            pltpu.sync_copy(there, here)

    dkv[:plain] = jnp.zeros_like(dkv[:plain])

    @pl.when(wide)
    def _():
        dkv[plain:] = jnp.zeros_like(dkv[plain:])

    @pl.when(pl.program_id(0) == 0)
    def _():
        for r in range(CORES):
            count = 0
            for b in range(n_blocks):
                order[r, count] = b
                count = count + info[2 + r * n_blocks + b]
            order[r, n_blocks] = count
            rpos = rinfo[r, 0]
            rseg = rinfo[r, 1]
            for b in range(n_blocks):
                kpos = kinfo[b, 0]
                kseg = kinfo[b, 1]
                seen = (kpos <= rpos) & ((kseg == rseg) | (kseg == 0))
                bias[r, b] = jnp.where(seen, 0.0, NEG)

    for r in range(CORES):
        for h in range(group):
            q_all[r, pl.ds(h * chunk, chunk), :] = q_refs[r][:, h * d : (h + 1) * d]
            g_all[r, pl.ds(h * chunk, chunk), :] = g_refs[r][:, h * d : (h + 1) * d]

    def one_chunk(r, carry):
        m_buf[...] = jnp.full_like(m_buf, NEG)

        def each(fn):
            def turn(i, carry):
                fn(order[r, i])
                return carry

            lax.fori_loop(0, order[r, n_blocks], turn, 0)

        def fold(op, t):
            return op(t.reshape(BLOCK // 8, 8, -1), axis=0)

        sub = min(rows, 256)
        tiles = [slice(i, i + sub) for i in range(0, rows, sub)]

        def score_pass(b):
            for t in tiles:
                s = dot(kv[b, :, :d], q_all[r, t], ((1,), (1,))) * log_scale
                s = s + jnp.concatenate([bias[r, b]] * (sub // bias.shape[3]), axis=1)
                s_buf[b, :, t] = s
                m_buf[:, t] = jnp.maximum(m_buf[:, t], fold(jnp.max, s))

        each(score_pass)
        m_buf[...] = jnp.broadcast_to(jnp.max(m_buf[...], axis=0, keepdims=True), m_buf.shape)
        l_buf[...] = jnp.zeros_like(l_buf)
        d_buf[...] = jnp.zeros_like(d_buf)
        acc[...] = jnp.zeros_like(acc)

        def weight_pass(b):
            for t in tiles:
                p = jnp.exp2(s_buf[b, :, t] - m_buf[0:1, t])
                dp = dot(kv[b, :, d:], g_all[r, t], ((1,), (1,)))
                dp_buf[b, :, t] = dp
                l_buf[:, t] += fold(jnp.sum, p)
                d_buf[:, t] += fold(jnp.sum, p * dp)
                acc[:, t] += dot(kv[b, :, d:], p.astype(BF16), ((0,), (0,)))

        each(weight_pass)
        inv = 1.0 / jnp.sum(l_buf[...], axis=0, keepdims=True)
        delta = jnp.sum(d_buf[...], axis=0, keepdims=True) * inv
        m_buf[...] = m_buf[...] - jnp.broadcast_to(jnp.log2(inv), m_buf.shape)
        d_buf[...] = jnp.broadcast_to(delta, d_buf.shape)
        o_all[r] = (acc[...] * inv).astype(BF16).T
        acc[...] = jnp.zeros_like(acc)

        def slope_pass(b):
            ds_low = []
            for i in range(0, BLOCK, 128):
                u = slice(i, i + 128)
                w = jnp.exp2(s_buf[b, u] - m_buf[0:1])
                ds = (w * (dp_buf[b, u] - d_buf[0:1])).astype(BF16)
                ds_low.append(ds)
                dkv[b, u, :d] += dot(ds, q_all[r], ((1,), (0,)))
                dkv[b, u, d:] += dot(w.astype(BF16), g_all[r], ((1,), (0,)))
            acc[...] += dot(kv[b, :, :d], jnp.concatenate(ds_low, axis=0), ((0,), (0,)))

        each(slope_pass)
        dq_all[r] = (acc[...] * scale).astype(BF16).T
        return carry

    lax.fori_loop(0, CORES, one_chunk, 0)
    for r in range(CORES):
        for h in range(group):
            o_refs[r][:, h * d : (h + 1) * d] = o_all[r, pl.ds(h * chunk, chunk), :]
            dq_refs[r][:, h * d : (h + 1) * d] = dq_all[r, pl.ds(h * chunk, chunk), :]

    def store(s, base, n):
        for b in range(n):
            for k in range(n_sub):
                rows_k = pl.ds(k * chunk, chunk)
                dkv_refs[s][k][b, :, :d] = (dkv[base + b, rows_k, :d] * scale).astype(BF16)
                dkv_refs[s][k][b, :, d:] = dkv[base + b, rows_k, d:].astype(BF16)

    for s, (base, n) in enumerate(parts[:-1]):
        store(s, base, n)

    @pl.when(wide)
    def _():
        kv[plain:, :, :d] = (dkv[plain:, :, :d] * scale).astype(BF16)
        kv[plain:, :, d:] = dkv[plain:, :, d:].astype(BF16)
        for k in range(n_sub):
            here, there = wide_part(dkv_refs[-1][k], k, head)
            pltpu.sync_copy(here, there)


def attention(call, info, kinfo, rinfo, mine, other, kv_sets, outs, group, heads):
    chunk = mine[0].shape[0]
    n_sub = len(kv_sets[0][1])
    all_heads = other[0].shape[1] // (group * HEAD_DIM)
    rows = group * chunk
    width = group * HEAD_DIM
    parts, n_blocks = [], 0
    for _, arrays in kv_sets:
        parts.append((n_blocks, arrays[0].shape[0]))
        n_blocks += arrays[0].shape[0]
    parts = tuple(parts)
    first = call * heads
    whole = lambda shape: pl.BlockSpec(shape, lambda h, info: (0,) * len(shape))
    mine_spec = pl.BlockSpec((chunk, width), lambda h, info: (0, info[0] * all_heads + first + h))
    other_spec = pl.BlockSpec((chunk, width), lambda h, info: (0, first + h))

    def kv_spec(n, column):
        return pl.BlockSpec((n, chunk, 2 * HEAD_DIM), lambda h, info: (0, 0, column + h))

    anywhere = pl.BlockSpec(memory_space=pl.ANY)

    in_specs = [whole(kinfo.shape), whole(rinfo.shape)] + [mine_spec, other_spec] * 2
    operands = [kinfo, rinfo, mine[0], other[0], mine[1], other[1]]
    for (column, arrays), (_, n) in zip(kv_sets[:-1], parts):
        in_specs += [kv_spec(n, column)] * n_sub
        operands += arrays
    in_specs += [anywhere] * n_sub
    operands += kv_sets[-1][1]
    aliases = {}
    if call:
        aliases = {1 + len(operands) + i: i for i in range(4)}
        in_specs += [anywhere] * 4
        operands += list(outs)
    full = jax.ShapeDtypeStruct(mine[0].shape, BF16)
    part = jax.ShapeDtypeStruct(other[0].shape, BF16)
    out_shape = [full, part, full, part]
    out_specs = [mine_spec, other_spec, mine_spec, other_spec]
    for s, (_, n) in enumerate(parts):
        out_shape += [jax.ShapeDtypeStruct((n, chunk, heads * 2 * HEAD_DIM), BF16)] * n_sub
        out_specs += [kv_spec(n, 0) if s < len(parts) - 1 else anywhere] * n_sub
    pairs = rows * 5 * BLOCK * CORES * heads
    results = pl.pallas_call(
        functools.partial(
            attention_kernel, n_sub, chunk, group, not call, kv_sets[-1][0], parts
        ),
        grid_spec=pltpu.PrefetchScalarGridSpec(
            num_scalar_prefetch=1,
            grid=(heads,),
            in_specs=in_specs,
            out_specs=out_specs,
            scratch_shapes=[
                pltpu.SMEM((CORES, n_blocks + 1), jnp.int32),
                pltpu.VMEM((n_blocks, BLOCK, 2 * HEAD_DIM), BF16),
                pltpu.VMEM((n_blocks, BLOCK, 2 * HEAD_DIM), F32),
                pltpu.VMEM((CORES, n_blocks, BLOCK, rinfo.shape[3]), F32),
                pltpu.VMEM((n_blocks, BLOCK, rows), F32),
                pltpu.VMEM((n_blocks, BLOCK, rows), F32),
                pltpu.VMEM((8, rows), F32),
                pltpu.VMEM((8, rows), F32),
                pltpu.VMEM((8, rows), F32),
                pltpu.VMEM((HEAD_DIM, rows), F32),
            ]
            + [pltpu.VMEM((CORES, rows, HEAD_DIM), BF16)] * 4,
        ),
        out_shape=out_shape,
        input_output_aliases=aliases,
        compiler_params=pltpu.CompilerParams(vmem_limit_bytes=56 << 20),
        cost_estimate=pl.CostEstimate(
            flops=12 * pairs * HEAD_DIM, bytes_accessed=8 << 20, transcendentals=pairs
        ),
        name=f"attention_{call}",
    )(info, *operands)
    grads = [results[4 + n_sub * i : 4 + n_sub * (i + 1)] for i in range(len(parts))]
    return results[:4], grads


def blank(shape):
    return pl.pallas_call(
        lambda out: None,
        out_shape=jax.ShapeDtypeStruct(shape, BF16),
        out_specs=pl.BlockSpec(memory_space=pl.ANY),
        name="blank",
    )()


def per_device(query_rows, key_rows, value_rows, out_grad, segment_ids):
    chunk = query_rows.shape[0]
    planes, n_sub = lax.axis_size("z"), lax.axis_size("x")
    halves = 2 * planes
    z, y, c, x = (lax.axis_index(a) for a in ALL)
    half = 2 * z + y
    devices = planes * 2 * CORES * n_sub
    kv_heads = key_rows.shape[1] // HEAD_DIM
    group = query_rows.shape[1] // key_rows.shape[1]
    my_heads = kv_heads // CORES
    heads = my_heads // SPLIT
    call_width = heads * 2 * HEAD_DIM

    def swap_cores(a):
        return lax.ppermute(a, "c", [(0, 1), (1, 0)])

    def rotate(a, by):
        return lax.ppermute(a, "x", [(i, (i + by) % n_sub) for i in range(n_sub)])

    def spread(a):
        return [a] + [rotate(a, k) for k in range(1, n_sub)]

    def send(a, by, k):
        moves = [
            (h * n_sub + i, (h + by) * n_sub + (i + k) % n_sub)
            for h in range(halves)
            if 0 <= h + by < halves
            for i in range(n_sub)
        ]
        return lax.ppermute(a, ("z", "y", "x"), moves)

    def gather_back(arrays):
        total = arrays[0].astype(F32)
        for k in range(1, n_sub):
            total = total + rotate(arrays[k], -k).astype(F32)
        return total

    def half_of(a, core):
        width = a.shape[1] // CORES
        return lax.dynamic_slice_in_dim(a, core * width, width, axis=1)

    def columns(core):
        k, v = half_of(key_rows, core), half_of(value_rows, core)
        cut = lambda a, h: a[:, h * HEAD_DIM : (h + 1) * HEAD_DIM]
        return jnp.concatenate([cut(a, h) for h in range(my_heads) for a in (k, v)], axis=1)

    kv_mine = columns(c)
    kv_other = swap_cores(columns(1 - c))
    kv_both = [
        jnp.stack([a[:, i * call_width : (i + 1) * call_width] for a in (kv_mine, kv_other)])
        for i in range(SPLIT)
    ]
    q_send, g_send, _ = lax.optimization_barrier(
        (half_of(query_rows, 1 - c), half_of(out_grad, 1 - c), kv_other)
    )
    q_other = swap_cores(q_send)
    g_other = swap_cores(g_send)
    segment_ids, _ = lax.optimization_barrier((segment_ids, kv_other))
    ids = lax.all_to_all(
        jnp.broadcast_to(segment_ids[None], (devices, chunk)), ALL, split_axis=0, concat_axis=0, tiled=True
    )
    n0 = jnp.sum((ids == 0).astype(jnp.int32))
    wide = n0 > BLOCK

    prompt = jnp.where(c == 0, kv_mine, kv_other)[None]
    step = halves // 2
    while step:
        got = lax.ppermute(prompt, ("z", "y"), [(i, i + step) for i in range(0, halves, 2 * step)])
        if step == halves // 2:
            got, q_other, g_other = lax.optimization_barrier((got, q_other, g_other))
        prompt = jnp.where(half % (2 * step) == step, got, prompt)
        step //= 2
    prompt_set = spread(prompt)

    def fetch_wide(_):
        moved = jnp.concatenate(kv_both, axis=2)
        step = planes // 2
        while step:
            got = lax.ppermute(moved, "z", [(i, i + step) for i in range(0, planes, 2 * step)])
            moved = jnp.where(z % (2 * step) == step, got, moved)
            step //= 2
        across = lax.ppermute(moved, "y", [(0, 1), (1, 0)])
        moved = jnp.concatenate([jnp.where(y == 0, moved, across), jnp.where(y == 0, across, moved)])
        return tuple(spread(moved))

    def no_wide(_):
        return tuple(blank((WIDE, chunk, SPLIT * call_width)) for _ in range(n_sub))

    wide_set = lax.cond(wide, fetch_wide, no_wide, 0)

    bands = []
    for a in kv_both:
        if bands:
            a, _ = lax.optimization_barrier((a, bands[-1]))
        bands.append([[send(a, by, k) if by or k else a for k in range(n_sub)] for by in range(3)])

    row_chunk = jnp.stack([(2 * half + (c ^ r)) * n_sub + x for r in range(CORES)])
    row_pos = row_chunk[:, None] * chunk + jnp.arange(chunk, dtype=jnp.int32)
    row_seg = jnp.take(ids, row_chunk, axis=0)
    rinfo = jnp.tile(jnp.stack([row_pos, row_seg], axis=1)[:, :, None], (1, 1, 1, pl.cdiv(128, chunk)))
    starts = jnp.sum((ids[None] < row_seg[:, :1, None]).astype(jnp.int32), axis=(1, 2))
    sub = (x - jnp.arange(n_sub, dtype=jnp.int32)) % n_sub
    block = jnp.stack(
        [2 * (half - s) + (c ^ k) for s in range(3) for k in range(CORES)]
        + [jnp.zeros((), jnp.int32), c, 1 - c, 2 + c, 3 - c]
    )
    place = jnp.arange(block.shape[0])
    usable = jnp.where(
        place < 6, block >= jnp.where(wide, WIDE, 1), jnp.where(place == 6, ~wide, wide)
    )
    key_chunk = jnp.clip(block, 0)[:, None] * n_sub + sub[None]
    key_seg = jnp.take(ids, key_chunk.reshape(-1), axis=0).reshape(-1, BLOCK)
    key_pos = (key_chunk[..., None] * chunk + jnp.arange(chunk, dtype=jnp.int32)).reshape(-1, BLOCK)
    key_pos = jnp.where(usable[:, None], key_pos, FAR)
    kinfo = jnp.stack([key_pos, key_seg], axis=1)[..., None]
    first = block * BLOCK
    need = (
        usable[None]
        & (first[None] <= row_pos[:, -1:])
        & ((first[None] < n0) | (first[None] + BLOCK > starts[:, None]))
    )
    info = jnp.concatenate(
        [jnp.stack([c, wide.astype(jnp.int32)]), need.astype(jnp.int32).reshape(-1)]
    )

    outs = None
    owns, prompts, wide_parts = [], [], []
    for i in range(SPLIT):
        column = heads * i
        sets = [(0, b) for b in bands[i]] + [(column, prompt_set), (column, wide_set)]
        outs, grads = attention(
            i, info, kinfo, rinfo, (query_rows, out_grad), (q_other, g_other), sets, outs, group, heads
        )
        if owns:
            (outs, grads), owns[-1] = lax.optimization_barrier(((outs, grads), owns[-1]))
        owns.append(
            [send(grads[by][k], -by, -k) if by or k else grads[0][0] for by in range(3) for k in range(n_sub)]
        )
        prompts.append(grads[3])
        wide_parts.append(tuple(grads[4]))

    back = gather_back([jnp.concatenate([p[k] for p in prompts], axis=2) for k in range(n_sub)])[0]
    step = 1
    while step < halves:
        got = lax.ppermute(
            back.astype(BF16), ("z", "y"), [(j + step, j) for j in range(0, halves, 2 * step)]
        )
        back = back + got.astype(F32)
        step *= 2
    mine = (jnp.arange(CORES) == c)[:, None, None] & (half == 0)
    total = jnp.where(mine, back[None], 0.0) + jnp.concatenate(
        [sum(a.astype(F32) for a in arrays) for arrays in owns], axis=2
    )

    def return_wide(parts):
        total = gather_back([jnp.concatenate([p[k] for p in parts], axis=2) for k in range(n_sub)])
        total = total.astype(BF16)
        keep = jnp.where(y == 0, total[:2], total[2:])
        send = jnp.where(y == 0, total[2:], total[:2])
        back = keep.astype(F32) + lax.ppermute(send, "y", [(0, 1), (1, 0)]).astype(F32)
        step = 1
        while step < planes:
            got = lax.ppermute(back.astype(BF16), "z", [(j + step, j) for j in range(0, planes, 2 * step)])
            back = back + got.astype(F32)
            step *= 2
        return jnp.where(z == 0, back, 0.0)

    total = lax.cond(
        wide,
        lambda t, parts: t + return_wide(parts),
        lambda t, parts: t,
        total,
        tuple(wide_parts),
    ).astype(BF16)

    got = swap_cores(total[1])
    low = jnp.where(c == 0, total[0], got)
    high = jnp.where(c == 0, got, total[0])

    def columns_back(t):
        starts = [(2 * h + t) * HEAD_DIM for h in range(my_heads)]
        return jnp.concatenate([a[:, s : s + HEAD_DIM] for a in (low, high) for s in starts], axis=1)

    def join(full, part):
        start = (1 - c) * part.shape[1]
        return lax.dynamic_update_slice(full, swap_cores(part), (0, start))

    return join(outs[0], outs[1]), join(outs[2], outs[3]), columns_back(0), columns_back(1)


def solution(mesh):
    blk, uly = mesh.shape["blk"], mesh.shape["uly"]
    parts = Mesh(np.asarray(mesh.devices).reshape(blk // 4, 2, CORES, uly), ALL)
    rows = P(ALL, None)
    return jax.shard_map(
        per_device,
        mesh=parts,
        in_specs=(rows, rows, rows, rows, P(ALL)),
        out_specs=(rows, rows, rows, rows),
        check_vma=False,
    )
```

```python
import functools
import math

import jax
import jax.numpy as jnp
import numpy as np
from jax import lax
from jax.experimental import pallas as pl
from jax.experimental.pallas import tpu as pltpu
from jax.sharding import Mesh
from jax.sharding import PartitionSpec as P

HEAD_DIM = 128
BLOCK = 256
WIDE = 4
NEG = -1e30
FAR = 1 << 30
ALL = ("z", "y", "c", "x")
CORES = 2
SPLIT = 2
F32 = jnp.float32
BF16 = jnp.bfloat16


def dot(a, b, dims):
    return lax.dot_general(a, b, (dims, ((), ())), preferred_element_type=F32)


def attention_kernel(n_sub, chunk, group, first_call, wide_column, parts, *refs):
    info, kinfo, rinfo = refs[:3]
    q_mine, g_mine, other = refs[3:6]
    at = 6
    kv_refs = []
    for _ in parts:
        kv_refs.append(refs[at : at + n_sub])
        at += n_sub
    if not first_call:
        at += 3
    o_mine, dq_mine, other_out = refs[at : at + 3]
    at += 3
    dkv_refs = []
    for _ in parts:
        dkv_refs.append(refs[at : at + n_sub])
        at += n_sub
    order, kv, dkv, bias, s_buf, dp_buf, m_buf, l_buf, d_buf, acc, q_all, g_all, o_all, dq_all = refs[at:]
    n_blocks = parts[-1][0] + parts[-1][1]
    rows = group * chunk
    scale = 1.0 / math.sqrt(HEAD_DIM)
    log_scale = scale * math.log2(math.e)
    d = HEAD_DIM
    wide = info[1] > 1

    def load(s):
        base, n = parts[s]
        for b in range(n):
            for k in range(n_sub):
                kv[base + b, pl.ds(k * chunk, chunk), :] = kv_refs[s][k][b]

    for s in range(len(parts) - 1):
        load(s)
    plain = parts[-1][0]
    head = pl.program_id(0)
    pair = 2 * d

    def wide_part(array, first, k, column):
        more = n_blocks - plain
        here = kv.at[pl.ds(plain, more), pl.ds(k * chunk, chunk), :]
        there = array.at[pl.ds(first, more), :, pl.ds(pl.multiple_of(column * pair, pair), pair)]
        return here, there

    @pl.when(wide)
    def _():
        for k in range(n_sub):
            here, there = wide_part(kv_refs[-1][k], 1, k, wide_column + head)
            pltpu.sync_copy(there, here)

    dkv[:plain] = jnp.zeros_like(dkv[:plain])

    @pl.when(wide)
    def _():
        dkv[plain:] = jnp.zeros_like(dkv[plain:])

    @pl.when(pl.program_id(0) == 0)
    def _():
        for r in range(CORES):
            count = 0
            for b in range(n_blocks):
                order[r, count] = b
                count = count + info[2 + r * n_blocks + b]
            order[r, n_blocks] = count
            rpos = rinfo[r, 0]
            rseg = rinfo[r, 1]
            for b in range(n_blocks):
                kpos = kinfo[b, 0]
                kseg = kinfo[b, 1]
                seen = (kpos <= rpos) & ((kseg == rseg) | (kseg == 0))
                bias[r, b] = jnp.where(seen, 0.0, NEG)

    for r in range(CORES):
        for h in range(group):
            here, columns = pl.ds(h * chunk, chunk), slice(h * d, (h + 1) * d)
            q_all[r, here, :] = other[0, :, columns] if r else q_mine[:, columns]
            g_all[r, here, :] = other[1, :, columns] if r else g_mine[:, columns]

    def one_chunk(r, carry):
        m_buf[...] = jnp.full_like(m_buf, NEG)

        def each(fn):
            def turn(i, carry):
                fn(order[r, i])
                return carry

            lax.fori_loop(0, order[r, n_blocks], turn, 0)

        def fold(op, t):
            return op(t.reshape(BLOCK // 8, 8, -1), axis=0)

        sub = min(rows, 256)
        tiles = [slice(i, i + sub) for i in range(0, rows, sub)]

        def score_pass(b):
            for t in tiles:
                s = dot(kv[b, :, :d], q_all[r, t], ((1,), (1,))) * log_scale
                s = s + jnp.concatenate([bias[r, b]] * (sub // bias.shape[3]), axis=1)
                s_buf[b, :, t] = s
                m_buf[:, t] = jnp.maximum(m_buf[:, t], fold(jnp.max, s))

        each(score_pass)
        m_buf[...] = jnp.broadcast_to(jnp.max(m_buf[...], axis=0, keepdims=True), m_buf.shape)
        l_buf[...] = jnp.zeros_like(l_buf)
        d_buf[...] = jnp.zeros_like(d_buf)
        acc[...] = jnp.zeros_like(acc)

        def weight_pass(b):
            for t in tiles:
                p = jnp.exp2(s_buf[b, :, t] - m_buf[0:1, t])
                dp = dot(kv[b, :, d:], g_all[r, t], ((1,), (1,)))
                dp_buf[b, :, t] = dp
                l_buf[:, t] += fold(jnp.sum, p)
                d_buf[:, t] += fold(jnp.sum, p * dp)
                acc[:, t] += dot(kv[b, :, d:], p.astype(BF16), ((0,), (0,)))

        each(weight_pass)
        inv = 1.0 / jnp.sum(l_buf[...], axis=0, keepdims=True)
        delta = jnp.sum(d_buf[...], axis=0, keepdims=True) * inv
        m_buf[...] = m_buf[...] - jnp.broadcast_to(jnp.log2(inv), m_buf.shape)
        d_buf[...] = jnp.broadcast_to(delta, d_buf.shape)
        o_all[r] = (acc[...] * inv).astype(BF16).T
        acc[...] = jnp.zeros_like(acc)

        def slope_pass(b):
            ds_low = []
            for i in range(0, BLOCK, 128):
                u = slice(i, i + 128)
                w = jnp.exp2(s_buf[b, u] - m_buf[0:1])
                ds = (w * (dp_buf[b, u] - d_buf[0:1])).astype(BF16)
                ds_low.append(ds)
                dkv[b, u, :d] += dot(ds, q_all[r], ((1,), (0,)))
                dkv[b, u, d:] += dot(w.astype(BF16), g_all[r], ((1,), (0,)))
            acc[...] += dot(kv[b, :, :d], jnp.concatenate(ds_low, axis=0), ((0,), (0,)))

        each(slope_pass)
        dq_all[r] = (acc[...] * scale).astype(BF16).T
        return carry

    lax.fori_loop(0, CORES, one_chunk, 0)
    for r in range(CORES):
        for h in range(group):
            here, columns = pl.ds(h * chunk, chunk), slice(h * d, (h + 1) * d)
            if r:
                other_out[0, :, columns] = o_all[r, here, :]
                other_out[1, :, columns] = dq_all[r, here, :]
            else:
                o_mine[:, columns] = o_all[r, here, :]
                dq_mine[:, columns] = dq_all[r, here, :]

    def store(s, base, n):
        for b in range(n):
            for k in range(n_sub):
                rows_k = pl.ds(k * chunk, chunk)
                dkv_refs[s][k][b, :, :d] = (dkv[base + b, rows_k, :d] * scale).astype(BF16)
                dkv_refs[s][k][b, :, d:] = dkv[base + b, rows_k, d:].astype(BF16)

    for s, (base, n) in enumerate(parts[:-1]):
        store(s, base, n)

    @pl.when(wide)
    def _():
        kv[plain:, :, :d] = (dkv[plain:, :, :d] * scale).astype(BF16)
        kv[plain:, :, d:] = dkv[plain:, :, d:].astype(BF16)
        for k in range(n_sub):
            here, there = wide_part(dkv_refs[-1][k], 0, k, head)
            pltpu.sync_copy(here, there)


def attention(call, info, kinfo, rinfo, mine, other, kv_sets, outs, group, heads):
    chunk = mine[0].shape[0]
    n_sub = len(kv_sets[0][1])
    all_heads = other.shape[2] // (group * HEAD_DIM)
    rows = group * chunk
    width = group * HEAD_DIM
    parts, n_blocks = [], 0
    for n in [a[0].shape[0] for _, a in kv_sets[:-1]] + [1, WIDE - 1]:
        parts.append((n_blocks, n))
        n_blocks += n
    parts = tuple(parts)
    first = call * heads
    whole = lambda shape: pl.BlockSpec(shape, lambda h, info: (0,) * len(shape))
    mine_spec = pl.BlockSpec((chunk, width), lambda h, info: (0, info[0] * all_heads + first + h))
    other_spec = pl.BlockSpec((2, chunk, width), lambda h, info: (0, 0, first + h))

    def kv_spec(n, column):
        return pl.BlockSpec((n, chunk, 2 * HEAD_DIM), lambda h, info: (0, 0, column + h))

    anywhere = pl.BlockSpec(memory_space=pl.ANY)

    in_specs = [whole(kinfo.shape), whole(rinfo.shape), mine_spec, mine_spec, other_spec]
    operands = [kinfo, rinfo, *mine, other]
    for (column, arrays), (_, n) in zip(kv_sets, parts):
        in_specs += [kv_spec(n, column)] * n_sub
        operands += arrays
    in_specs += [anywhere] * n_sub
    operands += kv_sets[-1][1]
    aliases = {}
    if call:
        aliases = {1 + len(operands) + i: i for i in range(3)}
        in_specs += [anywhere] * 3
        operands += list(outs)
    full = jax.ShapeDtypeStruct(mine[0].shape, BF16)
    out_shape = [full, full, jax.ShapeDtypeStruct(other.shape, BF16)]
    out_specs = [mine_spec, mine_spec, other_spec]
    for s, (_, n) in enumerate(parts):
        out_shape += [jax.ShapeDtypeStruct((n, chunk, heads * 2 * HEAD_DIM), BF16)] * n_sub
        out_specs += [kv_spec(n, 0) if s < len(parts) - 1 else anywhere] * n_sub
    pairs = rows * 5 * BLOCK * CORES * heads
    results = pl.pallas_call(
        functools.partial(
            attention_kernel, n_sub, chunk, group, not call, kv_sets[-1][0], parts
        ),
        grid_spec=pltpu.PrefetchScalarGridSpec(
            num_scalar_prefetch=1,
            grid=(heads,),
            in_specs=in_specs,
            out_specs=out_specs,
            scratch_shapes=[
                pltpu.SMEM((CORES, n_blocks + 1), jnp.int32),
                pltpu.VMEM((n_blocks, BLOCK, 2 * HEAD_DIM), BF16),
                pltpu.VMEM((n_blocks, BLOCK, 2 * HEAD_DIM), F32),
                pltpu.VMEM((CORES, n_blocks, BLOCK, rinfo.shape[3]), F32),
                pltpu.VMEM((n_blocks, BLOCK, rows), F32),
                pltpu.VMEM((n_blocks, BLOCK, rows), F32),
                pltpu.VMEM((8, rows), F32),
                pltpu.VMEM((8, rows), F32),
                pltpu.VMEM((8, rows), F32),
                pltpu.VMEM((HEAD_DIM, rows), F32),
            ]
            + [pltpu.VMEM((CORES, rows, HEAD_DIM), BF16)] * 4,
        ),
        out_shape=out_shape,
        input_output_aliases=aliases,
        compiler_params=pltpu.CompilerParams(vmem_limit_bytes=56 << 20),
        cost_estimate=pl.CostEstimate(
            flops=12 * pairs * HEAD_DIM, bytes_accessed=8 << 20, transcendentals=pairs
        ),
        name=f"attention_{call}",
    )(info, *operands)
    grads = [results[3 + n_sub * i : 3 + n_sub * (i + 1)] for i in range(len(parts))]
    return results[:3], grads


def blank(shape):
    return pl.pallas_call(
        lambda out: None,
        out_shape=jax.ShapeDtypeStruct(shape, BF16),
        out_specs=pl.BlockSpec(memory_space=pl.ANY),
        name="blank",
    )()


def per_device(query_rows, key_rows, value_rows, out_grad, segment_ids):
    chunk = query_rows.shape[0]
    planes, n_sub = lax.axis_size("z"), lax.axis_size("x")
    halves = 2 * planes
    z, y, c, x = (lax.axis_index(a) for a in ALL)
    half = 2 * z + y
    devices = planes * 2 * CORES * n_sub
    kv_heads = key_rows.shape[1] // HEAD_DIM
    group = query_rows.shape[1] // key_rows.shape[1]
    my_heads = kv_heads // CORES
    heads = my_heads // SPLIT
    call_width = heads * 2 * HEAD_DIM

    def swap_cores(a):
        return lax.ppermute(a, "c", [(0, 1), (1, 0)])

    def rotate(a, by):
        return lax.ppermute(a, "x", [(i, (i + by) % n_sub) for i in range(n_sub)])

    def spread(a):
        return [a] + [rotate(a, k) for k in range(1, n_sub)]

    def send(a, by, k):
        moves = [
            (h * n_sub + i, (h + by) * n_sub + (i + k) % n_sub)
            for h in range(halves)
            if 0 <= h + by < halves
            for i in range(n_sub)
        ]
        return lax.ppermute(a, ("z", "y", "x"), moves)

    def gather_back(arrays):
        total = arrays[0].astype(F32)
        for k in range(1, n_sub):
            total = total + rotate(arrays[k], -k).astype(F32)
        return total

    def half_of(a, core):
        width = a.shape[1] // CORES
        return lax.dynamic_slice_in_dim(a, core * width, width, axis=1)

    def columns(core):
        k, v = half_of(key_rows, core), half_of(value_rows, core)
        cut = lambda a, h: a[:, h * HEAD_DIM : (h + 1) * HEAD_DIM]
        return jnp.concatenate([cut(a, h) for h in range(my_heads) for a in (k, v)], axis=1)

    kv_mine = columns(c)
    kv_other = swap_cores(columns(1 - c))
    kv_pair = jnp.stack([kv_mine, kv_other])
    kv_both = [kv_pair[:, :, i * call_width : (i + 1) * call_width] for i in range(SPLIT)]
    other = swap_cores(jnp.stack([half_of(query_rows, 1 - c), half_of(out_grad, 1 - c)]))
    ids = lax.all_to_all(
        jnp.broadcast_to(segment_ids[None], (devices, chunk)), ALL, split_axis=0, concat_axis=0, tiled=True
    )
    n0 = jnp.sum((ids == 0).astype(jnp.int32))
    level = (n0 > BLOCK).astype(jnp.int32) + (n0 > 2 * BLOCK).astype(jnp.int32)
    count = jnp.left_shift(1, level)

    routes = [(by, k) for by in range(3) for k in range(n_sub)]

    def send_bands(a):
        sent = [send(a, *to) if any(to) else a for to in routes]
        return [sent[n_sub * by : n_sub * (by + 1)] for by in range(3)]

    def after(moved, sent, stage, stages):
        flat, tree_of = jax.tree.flatten(sent)
        part = len(flat) * stage // stages
        moved, flat[:part] = lax.optimization_barrier((moved, flat[:part]))
        return moved, jax.tree.unflatten(tree_of, flat)

    def return_bands(grads):
        return [send(grads[by][k], -by, -k) if by or k else grads[by][k] for by, k in routes]

    in_order = jnp.where(c == 0, kv_pair, kv_pair[::-1])

    def padded(arrays):
        room = blank((WIDE, chunk, SPLIT * call_width))
        return tuple(lax.dynamic_update_slice(room, a, (0, 0, 0)) for a in arrays)

    def fetch(blocks):
        def run(pair, band):
            moved = pair[:blocks]
            bands = send_bands(band)
            step, stages = halves // 2, halves.bit_length() - 1
            stage = 0
            while step:
                got = lax.ppermute(moved, ("z", "y"), [(i, i + step) for i in range(0, halves, 2 * step)])
                moved = jnp.where(half % (2 * step) == step, got, moved)
                step //= 2
                stage += 1
                moved, bands = after(moved, bands, stage, stages)
            return padded(spread(moved)), bands

        return run

    def fetch_all(moved, band):
        bands = send_bands(band)
        step = planes // 2
        while step:
            got = lax.ppermute(moved, "z", [(i, i + step) for i in range(0, planes, 2 * step)])
            moved = jnp.where(z % (2 * step) == step, got, moved)
            step //= 2
        across = lax.ppermute(moved, "y", [(0, 1), (1, 0)])
        moved = jnp.concatenate([jnp.where(y == 0, moved, across), jnp.where(y == 0, across, moved)])
        return tuple(spread(moved)), bands

    in_order, other = lax.optimization_barrier((in_order, other))
    prompt_set, first_bands = lax.switch(
        level, [fetch(1), fetch(2), fetch_all], in_order, kv_both[0]
    )
    bands = [first_bands]

    for a in kv_both[1:]:
        a, _, prompt_set = lax.optimization_barrier((a, bands[-1], prompt_set))
        bands.append(send_bands(a))

    row_chunk = jnp.stack([(2 * half + (c ^ r)) * n_sub + x for r in range(CORES)])
    row_pos = row_chunk[:, None] * chunk + jnp.arange(chunk, dtype=jnp.int32)
    row_seg = jnp.take(ids, row_chunk, axis=0)
    rinfo = jnp.tile(jnp.stack([row_pos, row_seg], axis=1)[:, :, None], (1, 1, 1, pl.cdiv(128, chunk)))
    starts = jnp.sum((ids[None] < row_seg[:, :1, None]).astype(jnp.int32), axis=(1, 2))
    sub = (x - jnp.arange(n_sub, dtype=jnp.int32)) % n_sub
    block = jnp.stack(
        [2 * (half - s) + (c ^ k) for s in range(3) for k in range(CORES)]
        + [jnp.full((), j, jnp.int32) for j in range(WIDE)]
    )
    place = jnp.arange(block.shape[0])
    usable = jnp.where(place < 6, block >= count, place - 6 < count)
    key_chunk = jnp.clip(block, 0)[:, None] * n_sub + sub[None]
    key_seg = jnp.take(ids, key_chunk.reshape(-1), axis=0).reshape(-1, BLOCK)
    key_pos = (key_chunk[..., None] * chunk + jnp.arange(chunk, dtype=jnp.int32)).reshape(-1, BLOCK)
    key_pos = jnp.where(usable[:, None], key_pos, FAR)
    kinfo = jnp.stack([key_pos, key_seg], axis=1)[..., None]
    first = block * BLOCK
    need = (
        usable[None]
        & (first[None] <= row_pos[:, -1:])
        & ((first[None] < n0) | (first[None] + BLOCK > starts[:, None]))
    )
    info = jnp.concatenate(
        [jnp.stack([c, count]), need.astype(jnp.int32).reshape(-1)]
    )

    outs = None
    owns, prompts, wide_parts = [], [], []
    for i in range(SPLIT):
        column = heads * i
        sets = [(0, b) for b in bands[i]] + [(column, prompt_set)]
        outs, grads = attention(
            i, info, kinfo, rinfo, (query_rows, out_grad), other, sets, outs, group, heads
        )
        if owns:
            (outs, grads), owns[-1] = lax.optimization_barrier(((outs, grads), owns[-1]))
        if i < SPLIT - 1:
            owns.append(return_bands(grads))
        prompts.append(tuple(grads[3]))
        wide_parts.append(tuple(grads[4]))

    joined = lambda parts, k: jnp.concatenate([p[k] for p in parts], axis=2)

    def tree(back, axes, length, beside):
        step, stage, stages = 1, 1, length.bit_length()
        while step < length:
            back, beside = after(back, beside, stage, stages)
            got = lax.ppermute(back.astype(BF16), axes, [(j + step, j) for j in range(0, length, 2 * step)])
            back = back + got.astype(F32)
            step *= 2
            stage += 1
        return back, beside

    def give_back(blocks):
        def run(parts, band, rows):
            own, arrived = return_bands(band), swap_cores(rows)
            arrays = []
            for k in range(n_sub):
                a = joined(parts[0], k)
                arrays.append(a if blocks == 1 else jnp.concatenate([a, joined(parts[1], k)[:1]]))
            back, (own, arrived) = tree(gather_back(arrays), ("z", "y"), halves, (own, arrived))
            if blocks == 1:
                back = jnp.where((jnp.arange(CORES) == c)[:, None, None], back, 0.0)
            else:
                back = jnp.where(c == 0, back, back[::-1])
            return jnp.where(half == 0, back, 0.0), own, arrived

        return run

    def give_all_back(parts, band, rows):
        own, arrived = return_bands(band), swap_cores(rows)
        back = gather_back(
            [jnp.concatenate([joined(parts[0], k), joined(parts[1], k)]) for k in range(n_sub)]
        ).astype(BF16)
        keep = jnp.where(y == 0, back[:2], back[2:])
        leave = jnp.where(y == 0, back[2:], back[:2])
        back = keep.astype(F32) + lax.ppermute(leave, "y", [(0, 1), (1, 0)]).astype(F32)
        back, (own, arrived) = tree(back, "z", planes, (own, arrived))
        back = jnp.where(c == 0, back, back[::-1])
        return jnp.where(z == 0, back, 0.0), own, arrived

    back, last_own, arrived = lax.switch(
        level,
        [give_back(1), give_back(2), give_all_back],
        (tuple(prompts), tuple(wide_parts)),
        grads[:3],
        outs[2],
    )
    owns.append(last_own)
    total = back + jnp.concatenate([sum(a.astype(F32) for a in arrays) for arrays in owns], axis=2)
    total = total.astype(BF16)

    got = swap_cores(total[1])
    low = jnp.where(c == 0, total[0], got)
    high = jnp.where(c == 0, got, total[0])

    def columns_back(t):
        starts = [(2 * h + t) * HEAD_DIM for h in range(my_heads)]
        return jnp.concatenate([a[:, s : s + HEAD_DIM] for a in (low, high) for s in starts], axis=1)

    def join(full, part):
        return lax.dynamic_update_slice(full, part, (0, (1 - c) * part.shape[1]))

    return join(outs[0], arrived[0]), join(outs[1], arrived[1]), columns_back(0), columns_back(1)


def solution(mesh):
    blk, uly = mesh.shape["blk"], mesh.shape["uly"]
    parts = Mesh(np.asarray(mesh.devices).reshape(blk // 4, 2, CORES, uly), ALL)
    rows = P(ALL, None)
    return jax.shard_map(
        per_device,
        mesh=parts,
        in_specs=(rows, rows, rows, rows, P(ALL)),
        out_specs=(rows, rows, rows, rows),
        check_vma=False,
    )
```

```python
import functools
import math

import jax
import jax.numpy as jnp
import numpy as np
from jax import lax
from jax.experimental import pallas as pl
from jax.experimental.pallas import tpu as pltpu
from jax.sharding import Mesh
from jax.sharding import PartitionSpec as P

HEAD_DIM = 128
BLOCK = 256
WIDE = 4
NEG = -1e30
FAR = 1 << 30
ALL = ("z", "y", "c", "x")
CORES = 2
SPLIT = 2
F32 = jnp.float32
BF16 = jnp.bfloat16


def dot(a, b, dims):
    return lax.dot_general(a, b, (dims, ((), ())), preferred_element_type=F32)


def attention_kernel(n_sub, chunk, group, first_call, wide_column, parts, *refs):
    info, kinfo, rinfo = refs[:3]
    q_mine, g_mine, other = refs[3:6]
    at = 6
    kv_refs = []
    for _ in parts:
        kv_refs.append(refs[at : at + n_sub])
        at += n_sub
    if not first_call:
        at += 3
    o_mine, dq_mine, other_out = refs[at : at + 3]
    at += 3
    dkv_refs = []
    for _ in parts:
        dkv_refs.append(refs[at : at + n_sub])
        at += n_sub
    order, kv, dkv, bias, s_buf, dp_buf, m_buf, l_buf, d_buf, acc, q_all, g_all, o_all, dq_all = refs[at:]
    n_blocks = parts[-1][0] + parts[-1][1]
    rows = group * chunk
    scale = 1.0 / math.sqrt(HEAD_DIM)
    log_scale = scale * math.log2(math.e)
    d = HEAD_DIM
    wide = info[1] > 1

    def load(s):
        base, n = parts[s]
        for b in range(n):
            for k in range(n_sub):
                for t in range(2):
                    kv[base + b, pl.ds(k * chunk, chunk), t * d : (t + 1) * d] = kv_refs[s][k][b, t]

    for s in range(len(parts) - 1):
        load(s)
    plain = parts[-1][0]
    head = pl.program_id(0)

    def wide_part(array, first, k, t, column):
        more = n_blocks - plain
        here = kv.at[pl.ds(plain, more), pl.ds(k * chunk, chunk), pl.ds(t * d, d)]
        there = array.at[pl.ds(first, more), t, :, pl.ds(pl.multiple_of(column * d, d), d)]
        return here, there

    @pl.when(wide)
    def _():
        for k in range(n_sub):
            for t in range(2):
                here, there = wide_part(kv_refs[-1][k], 1, k, t, wide_column + head)
                pltpu.sync_copy(there, here)

    dkv[:plain] = jnp.zeros_like(dkv[:plain])

    @pl.when(wide)
    def _():
        dkv[plain:] = jnp.zeros_like(dkv[plain:])

    @pl.when(pl.program_id(0) == 0)
    def _():
        for r in range(CORES):
            count = 0
            for b in range(n_blocks):
                order[r, count] = b
                count = count + info[2 + r * n_blocks + b]
            order[r, n_blocks] = count
            rpos = rinfo[r, 0]
            rseg = rinfo[r, 1]
            for b in range(n_blocks):
                kpos = kinfo[b, 0]
                kseg = kinfo[b, 1]
                seen = (kpos <= rpos) & ((kseg == rseg) | (kseg == 0))
                bias[r, b] = jnp.where(seen, 0.0, NEG)

    for r in range(CORES):
        for h in range(group):
            here, columns = pl.ds(h * chunk, chunk), slice(h * d, (h + 1) * d)
            q_all[r, here, :] = other[0, :, columns] if r else q_mine[:, columns]
            g_all[r, here, :] = other[1, :, columns] if r else g_mine[:, columns]

    def one_chunk(r, carry):
        m_buf[...] = jnp.full_like(m_buf, NEG)

        def each(fn):
            def turn(i, carry):
                fn(order[r, i])
                return carry

            lax.fori_loop(0, order[r, n_blocks], turn, 0)

        def fold(op, t):
            return op(t.reshape(BLOCK // 8, 8, -1), axis=0)

        sub = min(rows, 256)
        tiles = [slice(i, i + sub) for i in range(0, rows, sub)]

        def score_pass(b):
            for t in tiles:
                s = dot(kv[b, :, :d], q_all[r, t], ((1,), (1,))) * log_scale
                s = s + jnp.concatenate([bias[r, b]] * (sub // bias.shape[3]), axis=1)
                s_buf[b, :, t] = s
                m_buf[:, t] = jnp.maximum(m_buf[:, t], fold(jnp.max, s))

        each(score_pass)
        m_buf[...] = jnp.broadcast_to(jnp.max(m_buf[...], axis=0, keepdims=True), m_buf.shape)
        l_buf[...] = jnp.zeros_like(l_buf)
        d_buf[...] = jnp.zeros_like(d_buf)
        acc[...] = jnp.zeros_like(acc)

        def weight_pass(b):
            for t in tiles:
                p = jnp.exp2(s_buf[b, :, t] - m_buf[0:1, t])
                dp = dot(kv[b, :, d:], g_all[r, t], ((1,), (1,)))
                dp_buf[b, :, t] = dp
                l_buf[:, t] += fold(jnp.sum, p)
                d_buf[:, t] += fold(jnp.sum, p * dp)
                acc[:, t] += dot(kv[b, :, d:], p.astype(BF16), ((0,), (0,)))

        each(weight_pass)
        inv = 1.0 / jnp.sum(l_buf[...], axis=0, keepdims=True)
        delta = jnp.sum(d_buf[...], axis=0, keepdims=True) * inv
        m_buf[...] = m_buf[...] - jnp.broadcast_to(jnp.log2(inv), m_buf.shape)
        d_buf[...] = jnp.broadcast_to(delta, d_buf.shape)
        o_all[r] = (acc[...] * inv).astype(BF16).T
        acc[...] = jnp.zeros_like(acc)

        def slope_pass(b):
            ds_low = []
            for i in range(0, BLOCK, 128):
                u = slice(i, i + 128)
                w = jnp.exp2(s_buf[b, u] - m_buf[0:1])
                ds = (w * (dp_buf[b, u] - d_buf[0:1])).astype(BF16)
                ds_low.append(ds)
                dkv[b, u, :d] += dot(ds, q_all[r], ((1,), (0,)))
                dkv[b, u, d:] += dot(w.astype(BF16), g_all[r], ((1,), (0,)))
            acc[...] += dot(kv[b, :, :d], jnp.concatenate(ds_low, axis=0), ((0,), (0,)))

        each(slope_pass)
        dq_all[r] = (acc[...] * scale).astype(BF16).T
        return carry

    lax.fori_loop(0, CORES, one_chunk, 0)
    for r in range(CORES):
        for h in range(group):
            here, columns = pl.ds(h * chunk, chunk), slice(h * d, (h + 1) * d)
            if r:
                other_out[0, :, columns] = o_all[r, here, :]
                other_out[1, :, columns] = dq_all[r, here, :]
            else:
                o_mine[:, columns] = o_all[r, here, :]
                dq_mine[:, columns] = dq_all[r, here, :]

    def store(s, base, n):
        for b in range(n):
            for k in range(n_sub):
                rows_k = pl.ds(k * chunk, chunk)
                dkv_refs[s][k][b, 0] = (dkv[base + b, rows_k, :d] * scale).astype(BF16)
                dkv_refs[s][k][b, 1] = dkv[base + b, rows_k, d:].astype(BF16)

    for s, (base, n) in enumerate(parts[:-1]):
        store(s, base, n)

    @pl.when(wide)
    def _():
        kv[plain:, :, :d] = (dkv[plain:, :, :d] * scale).astype(BF16)
        kv[plain:, :, d:] = dkv[plain:, :, d:].astype(BF16)
        for k in range(n_sub):
            for t in range(2):
                here, there = wide_part(dkv_refs[-1][k], 0, k, t, head)
                pltpu.sync_copy(here, there)


def attention(call, info, kinfo, rinfo, mine, other, kv_sets, outs, group, heads):
    chunk = mine[0].shape[0]
    n_sub = len(kv_sets[0][1])
    all_heads = other.shape[2] // (group * HEAD_DIM)
    rows = group * chunk
    width = group * HEAD_DIM
    parts, n_blocks = [], 0
    for n in [a[0].shape[0] for _, a in kv_sets[:-1]] + [1, WIDE - 1]:
        parts.append((n_blocks, n))
        n_blocks += n
    parts = tuple(parts)
    first = call * heads
    whole = lambda shape: pl.BlockSpec(shape, lambda h, info: (0,) * len(shape))
    mine_spec = pl.BlockSpec((chunk, width), lambda h, info: (0, info[0] * all_heads + first + h))
    other_spec = pl.BlockSpec((2, chunk, width), lambda h, info: (0, 0, first + h))

    def kv_spec(n, column):
        return pl.BlockSpec((n, 2, chunk, HEAD_DIM), lambda h, info: (0, 0, 0, column + h))

    anywhere = pl.BlockSpec(memory_space=pl.ANY)

    in_specs = [whole(kinfo.shape), whole(rinfo.shape), mine_spec, mine_spec, other_spec]
    operands = [kinfo, rinfo, *mine, other]
    for (column, arrays), (_, n) in zip(kv_sets, parts):
        in_specs += [kv_spec(n, column)] * n_sub
        operands += arrays
    in_specs += [anywhere] * n_sub
    operands += kv_sets[-1][1]
    aliases = {}
    if call:
        aliases = {1 + len(operands) + i: i for i in range(3)}
        in_specs += [anywhere] * 3
        operands += list(outs)
    full = jax.ShapeDtypeStruct(mine[0].shape, BF16)
    out_shape = [full, full, jax.ShapeDtypeStruct(other.shape, BF16)]
    out_specs = [mine_spec, mine_spec, other_spec]
    for s, (_, n) in enumerate(parts):
        out_shape += [jax.ShapeDtypeStruct((n, 2, chunk, heads * HEAD_DIM), BF16)] * n_sub
        out_specs += [kv_spec(n, 0) if s < len(parts) - 1 else anywhere] * n_sub
    pairs = rows * 5 * BLOCK * CORES * heads
    results = pl.pallas_call(
        functools.partial(
            attention_kernel, n_sub, chunk, group, not call, kv_sets[-1][0], parts
        ),
        grid_spec=pltpu.PrefetchScalarGridSpec(
            num_scalar_prefetch=1,
            grid=(heads,),
            in_specs=in_specs,
            out_specs=out_specs,
            scratch_shapes=[
                pltpu.SMEM((CORES, n_blocks + 1), jnp.int32),
                pltpu.VMEM((n_blocks, BLOCK, 2 * HEAD_DIM), BF16),
                pltpu.VMEM((n_blocks, BLOCK, 2 * HEAD_DIM), F32),
                pltpu.VMEM((CORES, n_blocks, BLOCK, rinfo.shape[3]), F32),
                pltpu.VMEM((n_blocks, BLOCK, rows), F32),
                pltpu.VMEM((n_blocks, BLOCK, rows), F32),
                pltpu.VMEM((8, rows), F32),
                pltpu.VMEM((8, rows), F32),
                pltpu.VMEM((8, rows), F32),
                pltpu.VMEM((HEAD_DIM, rows), F32),
            ]
            + [pltpu.VMEM((CORES, rows, HEAD_DIM), BF16)] * 4,
        ),
        out_shape=out_shape,
        input_output_aliases=aliases,
        compiler_params=pltpu.CompilerParams(vmem_limit_bytes=56 << 20),
        cost_estimate=pl.CostEstimate(
            flops=12 * pairs * HEAD_DIM, bytes_accessed=8 << 20, transcendentals=pairs
        ),
        name=f"attention_{call}",
    )(info, *operands)
    grads = [results[3 + n_sub * i : 3 + n_sub * (i + 1)] for i in range(len(parts))]
    return results[:3], grads


def blank(shape):
    return pl.pallas_call(
        lambda out: None,
        out_shape=jax.ShapeDtypeStruct(shape, BF16),
        out_specs=pl.BlockSpec(memory_space=pl.ANY),
        name="blank",
    )()


def per_device(query_rows, key_rows, value_rows, out_grad, segment_ids):
    chunk = query_rows.shape[0]
    planes, n_sub = lax.axis_size("z"), lax.axis_size("x")
    halves = 2 * planes
    z, y, c, x = (lax.axis_index(a) for a in ALL)
    half = 2 * z + y
    devices = planes * 2 * CORES * n_sub
    kv_heads = key_rows.shape[1] // HEAD_DIM
    group = query_rows.shape[1] // key_rows.shape[1]
    my_heads = kv_heads // CORES
    heads = my_heads // SPLIT
    call_width = heads * HEAD_DIM

    def swap_cores(a):
        return lax.ppermute(a, "c", [(0, 1), (1, 0)])

    def rotate(a, by):
        return lax.ppermute(a, "x", [(i, (i + by) % n_sub) for i in range(n_sub)])

    def spread(a):
        return [a] + [rotate(a, k) for k in range(1, n_sub)]

    def send(a, by, k):
        moves = [
            (h * n_sub + i, (h + by) * n_sub + (i + k) % n_sub)
            for h in range(halves)
            if 0 <= h + by < halves
            for i in range(n_sub)
        ]
        return lax.ppermute(a, ("z", "y", "x"), moves)

    def gather_back(arrays):
        total = arrays[0].astype(F32)
        for k in range(1, n_sub):
            total = total + rotate(arrays[k], -k).astype(F32)
        return total

    def half_of(a, core):
        width = a.shape[1] // CORES
        return lax.dynamic_slice_in_dim(a, core * width, width, axis=1)

    def columns(core):
        return jnp.stack([half_of(key_rows, core), half_of(value_rows, core)])

    kv_send, segment_ids = lax.optimization_barrier((columns(1 - c), segment_ids))
    kv_pair = jnp.stack([columns(c), swap_cores(kv_send)])
    kv_both = [kv_pair[..., i * call_width : (i + 1) * call_width] for i in range(SPLIT)]
    rows_send = jnp.stack([half_of(query_rows, 1 - c), half_of(out_grad, 1 - c)])
    ids = lax.all_to_all(
        jnp.broadcast_to(segment_ids[None], (devices, chunk)), ALL, split_axis=0, concat_axis=0, tiled=True
    )
    n0 = jnp.sum((ids == 0).astype(jnp.int32))
    level = (n0 > BLOCK).astype(jnp.int32) + (n0 > 2 * BLOCK).astype(jnp.int32)

    routes = [(by, k) for by in range(3) for k in range(n_sub)]

    def send_bands(a):
        sent = [send(a, *to) if any(to) else a for to in routes]
        return [sent[n_sub * by : n_sub * (by + 1)] for by in range(3)]

    def after(moved, sent, stage, stages):
        flat, tree_of = jax.tree.flatten(sent)
        part = len(flat) * stage // stages
        moved, flat[:part] = lax.optimization_barrier((moved, flat[:part]))
        return moved, jax.tree.unflatten(tree_of, flat)

    def return_bands(grads):
        return [send(grads[by][k], -by, -k) if by or k else grads[by][k] for by, k in routes]

    in_order = jnp.where(c == 0, kv_pair, kv_pair[::-1])

    def describe(ids, n0, count):
        row_chunk = jnp.stack([(2 * half + (c ^ r)) * n_sub + x for r in range(CORES)])
        row_pos = row_chunk[:, None] * chunk + jnp.arange(chunk, dtype=jnp.int32)
        row_seg = jnp.take(ids, row_chunk, axis=0)
        rinfo = jnp.tile(jnp.stack([row_pos, row_seg], axis=1)[:, :, None], (1, 1, 1, pl.cdiv(128, chunk)))
        starts = jnp.sum((ids[None] < row_seg[:, :1, None]).astype(jnp.int32), axis=(1, 2))
        sub = (x - jnp.arange(n_sub, dtype=jnp.int32)) % n_sub
        block = jnp.stack(
            [2 * (half - s) + (c ^ k) for s in range(3) for k in range(CORES)]
            + [jnp.full((), j, jnp.int32) for j in range(WIDE)]
        )
        place = jnp.arange(block.shape[0])
        usable = jnp.where(place < 6, block >= count, place - 6 < count)
        key_chunk = jnp.clip(block, 0)[:, None] * n_sub + sub[None]
        key_seg = jnp.take(ids, key_chunk.reshape(-1), axis=0).reshape(-1, BLOCK)
        key_pos = (key_chunk[..., None] * chunk + jnp.arange(chunk, dtype=jnp.int32)).reshape(-1, BLOCK)
        key_pos = jnp.where(usable[:, None], key_pos, FAR)
        kinfo = jnp.stack([key_pos, key_seg], axis=1)[..., None]
        first = block * BLOCK
        need = (
            usable[None]
            & (first[None] <= row_pos[:, -1:])
            & ((first[None] < n0) | (first[None] + BLOCK > starts[:, None]))
        )
        info = jnp.concatenate(
            [jnp.stack([c, jnp.full((), count, c.dtype)]), need.astype(jnp.int32).reshape(-1)]
        )
        return info, kinfo, rinfo

    def padded(arrays):
        room = blank((WIDE, 2, chunk, SPLIT * call_width))
        return tuple(lax.dynamic_update_slice(room, a, (0, 0, 0, 0)) for a in arrays)

    def fetch(blocks):
        def run(pair, band, rows, ids, n0):
            moved = pair[:blocks]
            bands = (send_bands(band), swap_cores(rows))
            step, stages = halves // 2, halves.bit_length() - 1
            stage = 0
            while step:
                got = lax.ppermute(moved, ("z", "y"), [(i, i + step) for i in range(0, halves, 2 * step)])
                moved = jnp.where(half % (2 * step) == step, got, moved)
                step //= 2
                stage += 1
                moved, bands = after(moved, bands, stage, stages)
            return padded(spread(moved)), bands, describe(ids, n0, blocks)

        return run

    def fetch_all(moved, band, rows, ids, n0):
        bands = (send_bands(band), swap_cores(rows))
        step = planes // 2
        while step:
            got = lax.ppermute(moved, "z", [(i, i + step) for i in range(0, planes, 2 * step)])
            moved = jnp.where(z % (2 * step) == step, got, moved)
            step //= 2
        across = lax.ppermute(moved, "y", [(0, 1), (1, 0)])
        moved = jnp.concatenate([jnp.where(y == 0, moved, across), jnp.where(y == 0, across, moved)])
        return tuple(spread(moved)), bands, describe(ids, n0, WIDE)

    prompt_set, (first_bands, other), (info, kinfo, rinfo) = lax.switch(
        level, [fetch(1), fetch(2), fetch_all], in_order, kv_both[0], rows_send, ids, n0
    )
    bands = [first_bands]

    for a in kv_both[1:]:
        a, _, prompt_set = lax.optimization_barrier((a, bands[-1], prompt_set))
        bands.append(send_bands(a))

    outs = None
    owns, prompts, wide_parts = [], [], []
    for i in range(SPLIT):
        column = heads * i
        sets = [(0, b) for b in bands[i]] + [(column, prompt_set)]
        outs, grads = attention(
            i, info, kinfo, rinfo, (query_rows, out_grad), other, sets, outs, group, heads
        )
        if owns:
            (outs, grads), owns[-1] = lax.optimization_barrier(((outs, grads), owns[-1]))
        if i < SPLIT - 1:
            owns.append(return_bands(grads))
        prompts.append(tuple(grads[3]))
        wide_parts.append(tuple(grads[4]))

    joined = lambda parts, k: jnp.concatenate([p[k] for p in parts], axis=3)

    def tree(back, axes, length, beside):
        step, stage, stages = 1, 1, length.bit_length()
        while step < length:
            back, beside = after(back, beside, stage, stages)
            got = lax.ppermute(back.astype(BF16), axes, [(j + step, j) for j in range(0, length, 2 * step)])
            back = back + got.astype(F32)
            step *= 2
            stage += 1
        return back, beside

    def give_back(blocks):
        def run(parts, band, rows):
            own, arrived = return_bands(band), swap_cores(rows)
            arrays = []
            for k in range(n_sub):
                a = joined(parts[0], k)
                arrays.append(a if blocks == 1 else jnp.concatenate([a, joined(parts[1], k)[:1]]))
            back, (own, arrived) = tree(gather_back(arrays), ("z", "y"), halves, (own, arrived))
            if blocks == 1:
                back = jnp.where((jnp.arange(CORES) == c)[:, None, None, None], back, 0.0)
            else:
                back = jnp.where(c == 0, back, back[::-1])
            return jnp.where(half == 0, back, 0.0), own, arrived

        return run

    def give_all_back(parts, band, rows):
        own, arrived = return_bands(band), swap_cores(rows)
        back = gather_back(
            [jnp.concatenate([joined(parts[0], k), joined(parts[1], k)]) for k in range(n_sub)]
        ).astype(BF16)
        keep = jnp.where(y == 0, back[:2], back[2:])
        leave = jnp.where(y == 0, back[2:], back[:2])
        back = keep.astype(F32) + lax.ppermute(leave, "y", [(0, 1), (1, 0)]).astype(F32)
        back, (own, arrived) = tree(back, "z", planes, (own, arrived))
        back = jnp.where(c == 0, back, back[::-1])
        return jnp.where(z == 0, back, 0.0), own, arrived

    back, last_own, arrived = lax.switch(
        level,
        [give_back(1), give_back(2), give_all_back],
        (tuple(prompts), tuple(wide_parts)),
        grads[:3],
        outs[2],
    )
    owns.append(last_own)
    total = back + jnp.concatenate([sum(a.astype(F32) for a in arrays) for arrays in owns], axis=3)
    total = total.astype(BF16)

    got = swap_cores(total[1])
    low = jnp.where(c == 0, total[0], got)
    high = jnp.where(c == 0, got, total[0])

    def columns_back(t):
        return jnp.concatenate([low[t], high[t]], axis=1)

    def join(full, part):
        return lax.dynamic_update_slice(full, part, (0, (1 - c) * part.shape[1]))

    return join(outs[0], arrived[0]), join(outs[1], arrived[1]), columns_back(0), columns_back(1)


def solution(mesh):
    blk, uly = mesh.shape["blk"], mesh.shape["uly"]
    parts = Mesh(np.asarray(mesh.devices).reshape(blk // 4, 2, CORES, uly), ALL)
    rows = P(ALL, None)
    return jax.shard_map(
        per_device,
        mesh=parts,
        in_specs=(rows, rows, rows, rows, P(ALL)),
        out_specs=(rows, rows, rows, rows),
        check_vma=False,
    )
```

```python
import functools
import math

import jax
import jax.numpy as jnp
import numpy as np
from jax import lax
from jax.experimental import pallas as pl
from jax.experimental.pallas import tpu as pltpu
from jax.sharding import Mesh
from jax.sharding import PartitionSpec as P

HEAD_DIM = 128
BLOCK = 256
WIDE = 4
NEG = -1e30
FAR = 1 << 30
ALL = ("z", "y", "c", "x")
CORES = 2
SPLIT = 2
F32 = jnp.float32
BF16 = jnp.bfloat16


def dot(a, b, dims):
    return lax.dot_general(a, b, (dims, ((), ())), preferred_element_type=F32)


def attention_kernel(n_sub, chunk, group, first_call, wide_column, parts, *refs):
    info, kinfo, rinfo = refs[:3]
    q_mine, g_mine, other = refs[3:6]
    at = 6
    kv_refs = []
    for _ in parts:
        kv_refs.append(refs[at : at + n_sub])
        at += n_sub
    if not first_call:
        at += 3
    o_mine, dq_mine, other_out = refs[at : at + 3]
    at += 3
    dkv_refs = []
    for _ in parts:
        dkv_refs.append(refs[at : at + n_sub])
        at += n_sub
    order, kv, dkv, bias, s_buf, dp_buf, m_buf, l_buf, d_buf, acc, q_all, g_all, o_all, dq_all = refs[at:]
    n_blocks = parts[-1][0] + parts[-1][1]
    rows = group * chunk
    scale = 1.0 / math.sqrt(HEAD_DIM)
    log_scale = scale * math.log2(math.e)
    d = HEAD_DIM
    wide = info[1] > 1

    def load(s):
        base, n = parts[s]
        for b in range(n):
            for k in range(n_sub):
                for t in range(2):
                    kv[base + b, pl.ds(k * chunk, chunk), t * d : (t + 1) * d] = kv_refs[s][k][b, t]

    for s in range(len(parts) - 1):
        load(s)
    plain = parts[-1][0]
    head = pl.program_id(0)

    def wide_part(array, first, k, t, column):
        more = n_blocks - plain
        here = kv.at[pl.ds(plain, more), pl.ds(k * chunk, chunk), pl.ds(t * d, d)]
        there = array.at[pl.ds(first, more), t, :, pl.ds(pl.multiple_of(column * d, d), d)]
        return here, there

    @pl.when(wide)
    def _():
        for k in range(n_sub):
            for t in range(2):
                here, there = wide_part(kv_refs[-1][k], 1, k, t, wide_column + head)
                pltpu.sync_copy(there, here)

    dkv[:plain] = jnp.zeros_like(dkv[:plain])

    @pl.when(wide)
    def _():
        dkv[plain:] = jnp.zeros_like(dkv[plain:])

    @pl.when(pl.program_id(0) == 0)
    def _():
        for r in range(CORES):
            count = 0
            for b in range(n_blocks):
                order[r, count] = b
                count = count + info[2 + r * n_blocks + b]
            order[r, n_blocks] = count
            rpos = rinfo[r, 0]
            rseg = rinfo[r, 1]
            for b in range(n_blocks):
                kpos = kinfo[b, 0]
                kseg = kinfo[b, 1]
                seen = (kpos <= rpos) & ((kseg == rseg) | (kseg == 0))
                bias[r, b] = jnp.where(seen, 0.0, NEG)

    for r in range(CORES):
        for h in range(group):
            here, columns = pl.ds(h * chunk, chunk), slice(h * d, (h + 1) * d)
            q_all[r, here, :] = other[0, :, columns] if r else q_mine[:, columns]
            g_all[r, here, :] = other[1, :, columns] if r else g_mine[:, columns]

    def one_chunk(r, carry):
        m_buf[...] = jnp.full_like(m_buf, NEG)

        def each(fn):
            def turn(i, carry):
                fn(order[r, i])
                return carry

            lax.fori_loop(0, order[r, n_blocks], turn, 0)

        def fold(op, t):
            return op(t.reshape(BLOCK // 8, 8, -1), axis=0)

        sub = min(rows, 256)
        tiles = [slice(i, i + sub) for i in range(0, rows, sub)]

        def score_pass(b):
            for t in tiles:
                s = dot(kv[b, :, :d], q_all[r, t], ((1,), (1,))) * log_scale
                s = s + jnp.concatenate([bias[r, b]] * (sub // bias.shape[3]), axis=1)
                s_buf[b, :, t] = s
                m_buf[:, t] = jnp.maximum(m_buf[:, t], fold(jnp.max, s))

        each(score_pass)
        m_buf[...] = jnp.broadcast_to(jnp.max(m_buf[...], axis=0, keepdims=True), m_buf.shape)
        l_buf[...] = jnp.zeros_like(l_buf)
        d_buf[...] = jnp.zeros_like(d_buf)
        acc[...] = jnp.zeros_like(acc)

        def weight_pass(b):
            for t in tiles:
                p = jnp.exp2(s_buf[b, :, t] - m_buf[0:1, t])
                dp = dot(kv[b, :, d:], g_all[r, t], ((1,), (1,)))
                dp_buf[b, :, t] = dp
                l_buf[:, t] += fold(jnp.sum, p)
                d_buf[:, t] += fold(jnp.sum, p * dp)
                acc[:, t] += dot(kv[b, :, d:], p.astype(BF16), ((0,), (0,)))

        each(weight_pass)
        inv = 1.0 / jnp.sum(l_buf[...], axis=0, keepdims=True)
        delta = jnp.sum(d_buf[...], axis=0, keepdims=True) * inv
        m_buf[...] = m_buf[...] - jnp.broadcast_to(jnp.log2(inv), m_buf.shape)
        d_buf[...] = jnp.broadcast_to(delta, d_buf.shape)
        o_all[r] = (acc[...] * inv).astype(BF16).T
        acc[...] = jnp.zeros_like(acc)

        def slope_pass(b):
            ds_low = []
            for i in range(0, BLOCK, 128):
                u = slice(i, i + 128)
                w = jnp.exp2(s_buf[b, u] - m_buf[0:1])
                ds = (w * (dp_buf[b, u] - d_buf[0:1])).astype(BF16)
                ds_low.append(ds)
                dkv[b, u, :d] += dot(ds, q_all[r], ((1,), (0,)))
                dkv[b, u, d:] += dot(w.astype(BF16), g_all[r], ((1,), (0,)))
            acc[...] += dot(kv[b, :, :d], jnp.concatenate(ds_low, axis=0), ((0,), (0,)))

        each(slope_pass)
        dq_all[r] = (acc[...] * scale).astype(BF16).T
        return carry

    lax.fori_loop(0, CORES, one_chunk, 0)
    for r in range(CORES):
        for h in range(group):
            here, columns = pl.ds(h * chunk, chunk), slice(h * d, (h + 1) * d)
            if r:
                other_out[0, :, columns] = o_all[r, here, :]
                other_out[1, :, columns] = dq_all[r, here, :]
            else:
                o_mine[:, columns] = o_all[r, here, :]
                dq_mine[:, columns] = dq_all[r, here, :]

    def store(s, base, n):
        for b in range(n):
            for k in range(n_sub):
                rows_k = pl.ds(k * chunk, chunk)
                dkv_refs[s][k][b, 0] = (dkv[base + b, rows_k, :d] * scale).astype(BF16)
                dkv_refs[s][k][b, 1] = dkv[base + b, rows_k, d:].astype(BF16)

    for s, (base, n) in enumerate(parts[:-1]):
        store(s, base, n)

    @pl.when(wide)
    def _():
        kv[plain:, :, :d] = (dkv[plain:, :, :d] * scale).astype(BF16)
        kv[plain:, :, d:] = dkv[plain:, :, d:].astype(BF16)
        for k in range(n_sub):
            for t in range(2):
                here, there = wide_part(dkv_refs[-1][k], 0, k, t, head)
                pltpu.sync_copy(here, there)


def attention(call, info, kinfo, rinfo, mine, other, kv_sets, outs, group, heads):
    chunk = mine[0].shape[0]
    n_sub = len(kv_sets[0][1])
    all_heads = other.shape[2] // (group * HEAD_DIM)
    rows = group * chunk
    width = group * HEAD_DIM
    parts, n_blocks = [], 0
    for n in [a[0].shape[0] for _, a in kv_sets[:-1]] + [1, WIDE - 1]:
        parts.append((n_blocks, n))
        n_blocks += n
    parts = tuple(parts)
    first = call * heads
    whole = lambda shape: pl.BlockSpec(shape, lambda h, info: (0,) * len(shape))
    mine_spec = pl.BlockSpec((chunk, width), lambda h, info: (0, info[0] * all_heads + first + h))
    other_spec = pl.BlockSpec((2, chunk, width), lambda h, info: (0, 0, first + h))

    def kv_spec(n, column):
        return pl.BlockSpec((n, 2, chunk, HEAD_DIM), lambda h, info: (0, 0, 0, column + h))

    anywhere = pl.BlockSpec(memory_space=pl.ANY)

    in_specs = [whole(kinfo.shape), whole(rinfo.shape), mine_spec, mine_spec, other_spec]
    operands = [kinfo, rinfo, *mine, other]
    for (column, arrays), (_, n) in zip(kv_sets, parts):
        in_specs += [kv_spec(n, column)] * n_sub
        operands += arrays
    in_specs += [anywhere] * n_sub
    operands += kv_sets[-1][1]
    aliases = {}
    if call:
        aliases = {1 + len(operands) + i: i for i in range(3)}
        in_specs += [anywhere] * 3
        operands += list(outs)
    full = jax.ShapeDtypeStruct(mine[0].shape, BF16)
    out_shape = [full, full, jax.ShapeDtypeStruct(other.shape, BF16)]
    out_specs = [mine_spec, mine_spec, other_spec]
    for s, (_, n) in enumerate(parts):
        out_shape += [jax.ShapeDtypeStruct((n, 2, chunk, heads * HEAD_DIM), BF16)] * n_sub
        out_specs += [kv_spec(n, 0) if s < len(parts) - 1 else anywhere] * n_sub
    pairs = rows * 5 * BLOCK * CORES * heads
    results = pl.pallas_call(
        functools.partial(
            attention_kernel, n_sub, chunk, group, not call, kv_sets[-1][0], parts
        ),
        grid_spec=pltpu.PrefetchScalarGridSpec(
            num_scalar_prefetch=1,
            grid=(heads,),
            in_specs=in_specs,
            out_specs=out_specs,
            scratch_shapes=[
                pltpu.SMEM((CORES, n_blocks + 1), jnp.int32),
                pltpu.VMEM((n_blocks, BLOCK, 2 * HEAD_DIM), BF16),
                pltpu.VMEM((n_blocks, BLOCK, 2 * HEAD_DIM), F32),
                pltpu.VMEM((CORES, n_blocks, BLOCK, rinfo.shape[3]), F32),
                pltpu.VMEM((n_blocks, BLOCK, rows), F32),
                pltpu.VMEM((n_blocks, BLOCK, rows), F32),
                pltpu.VMEM((8, rows), F32),
                pltpu.VMEM((8, rows), F32),
                pltpu.VMEM((8, rows), F32),
                pltpu.VMEM((HEAD_DIM, rows), F32),
            ]
            + [pltpu.VMEM((CORES, rows, HEAD_DIM), BF16)] * 4,
        ),
        out_shape=out_shape,
        input_output_aliases=aliases,
        compiler_params=pltpu.CompilerParams(vmem_limit_bytes=56 << 20),
        cost_estimate=pl.CostEstimate(
            flops=12 * pairs * HEAD_DIM, bytes_accessed=8 << 20, transcendentals=pairs
        ),
        name=f"attention_{call}",
    )(info, *operands)
    grads = [results[3 + n_sub * i : 3 + n_sub * (i + 1)] for i in range(len(parts))]
    return results[:3], grads


def blank(shape):
    return pl.pallas_call(
        lambda out: None,
        out_shape=jax.ShapeDtypeStruct(shape, BF16),
        out_specs=pl.BlockSpec(memory_space=pl.ANY),
        name="blank",
    )()


def per_device(query_rows, key_rows, value_rows, out_grad, segment_ids):
    chunk = query_rows.shape[0]
    planes, n_sub = lax.axis_size("z"), lax.axis_size("x")
    halves = 2 * planes
    z, y, c, x = (lax.axis_index(a) for a in ALL)
    half = 2 * z + y
    devices = planes * 2 * CORES * n_sub
    kv_heads = key_rows.shape[1] // HEAD_DIM
    group = query_rows.shape[1] // key_rows.shape[1]
    my_heads = kv_heads // CORES
    heads = my_heads // SPLIT
    call_width = heads * HEAD_DIM

    def swap_cores(a):
        return lax.ppermute(a, "c", [(0, 1), (1, 0)])

    def rotate(a, by):
        return lax.ppermute(a, "x", [(i, (i + by) % n_sub) for i in range(n_sub)])

    def spread(a):
        return [a] + [rotate(a, k) for k in range(1, n_sub)]

    def send(a, by, k):
        moves = [
            (h * n_sub + i, (h + by) * n_sub + (i + k) % n_sub)
            for h in range(halves)
            if 0 <= h + by < halves
            for i in range(n_sub)
        ]
        return lax.ppermute(a, ("z", "y", "x"), moves)

    def gather_back(arrays):
        total = arrays[0].astype(F32)
        for k in range(1, n_sub):
            total = total + rotate(arrays[k], -k).astype(F32)
        return total

    def half_of(a, core):
        width = a.shape[1] // CORES
        return lax.dynamic_slice_in_dim(a, core * width, width, axis=1)

    def columns(core):
        return jnp.stack([half_of(key_rows, core), half_of(value_rows, core)])

    kv_send, segment_ids = lax.optimization_barrier((columns(1 - c), segment_ids))
    kv_pair = jnp.stack([columns(c), swap_cores(kv_send)])
    kv_both = [kv_pair[..., i * call_width : (i + 1) * call_width] for i in range(SPLIT)]
    rows_send = jnp.stack([half_of(query_rows, 1 - c), half_of(out_grad, 1 - c)])
    ids = lax.all_to_all(
        jnp.broadcast_to(segment_ids[None], (devices, chunk)), ALL, split_axis=0, concat_axis=0, tiled=True
    )
    n0 = jnp.sum((ids == 0).astype(jnp.int32))
    level = (n0 > BLOCK).astype(jnp.int32) + (n0 > 2 * BLOCK).astype(jnp.int32)

    routes = [(by, k) for by in range(3) for k in range(n_sub)]

    def send_bands(a):
        sent = [send(a, *to) if any(to) else a for to in routes]
        return [sent[n_sub * by : n_sub * (by + 1)] for by in range(3)]

    def after(moved, sent, stage, stages):
        flat, tree_of = jax.tree.flatten(sent)
        part = len(flat) * stage // stages
        moved, flat[:part] = lax.optimization_barrier((moved, flat[:part]))
        return moved, jax.tree.unflatten(tree_of, flat)

    def stage_bands(a, rows):
        near = [send(a, by, 0) for by in (1, 2)]
        moved = [[rotate(b, k) for k in range(1, n_sub)] for b in [a] + near]
        return near, moved, swap_cores(rows)

    def unstage(a, staged):
        near, moved, other = staged
        return [[b] + m for b, m in zip([a] + near, moved)], other

    def stage_return(grads, rows):
        moved = [[rotate(g[k], -k) for k in range(1, n_sub)] for g in (grads[1], grads[2], grads[0])]
        near = []
        for by in (1, 2):
            total = sum((a.astype(F32) for a in moved[by - 1]), grads[by][0].astype(F32))
            near.append(send(total.astype(BF16), -by, 0))
        return moved, near, swap_cores(rows)

    def return_bands(grads):
        return [send(grads[by][k], -by, -k) if by or k else grads[by][k] for by, k in routes]

    in_order = jnp.where(c == 0, kv_pair, kv_pair[::-1])

    def describe(ids, n0, count):
        row_chunk = jnp.stack([(2 * half + (c ^ r)) * n_sub + x for r in range(CORES)])
        row_pos = row_chunk[:, None] * chunk + jnp.arange(chunk, dtype=jnp.int32)
        row_seg = jnp.take(ids, row_chunk, axis=0)
        rinfo = jnp.tile(jnp.stack([row_pos, row_seg], axis=1)[:, :, None], (1, 1, 1, pl.cdiv(128, chunk)))
        starts = jnp.sum((ids[None] < row_seg[:, :1, None]).astype(jnp.int32), axis=(1, 2))
        sub = (x - jnp.arange(n_sub, dtype=jnp.int32)) % n_sub
        block = jnp.stack(
            [2 * (half - s) + (c ^ k) for s in range(3) for k in range(CORES)]
            + [jnp.full((), j, jnp.int32) for j in range(WIDE)]
        )
        place = jnp.arange(block.shape[0])
        usable = jnp.where(place < 6, block >= count, place - 6 < count)
        key_chunk = jnp.clip(block, 0)[:, None] * n_sub + sub[None]
        key_seg = jnp.take(ids, key_chunk.reshape(-1), axis=0).reshape(-1, BLOCK)
        key_pos = (key_chunk[..., None] * chunk + jnp.arange(chunk, dtype=jnp.int32)).reshape(-1, BLOCK)
        key_pos = jnp.where(usable[:, None], key_pos, FAR)
        kinfo = jnp.stack([key_pos, key_seg], axis=1)[..., None]
        first = block * BLOCK
        need = (
            usable[None]
            & (first[None] <= row_pos[:, -1:])
            & ((first[None] < n0) | (first[None] + BLOCK > starts[:, None]))
        )
        info = jnp.concatenate(
            [jnp.stack([c, jnp.full((), count, c.dtype)]), need.astype(jnp.int32).reshape(-1)]
        )
        return info, kinfo, rinfo

    def padded(arrays):
        room = blank((WIDE, 2, chunk, SPLIT * call_width))
        return tuple(lax.dynamic_update_slice(room, a, (0, 0, 0, 0)) for a in arrays)

    def fetch(blocks):
        def run(pair, band, rows, ids, n0):
            moved = pair[:blocks]
            bands = stage_bands(band, rows)
            step, stages = halves // 2, halves.bit_length() - 1
            stage = 0
            while step:
                got = lax.ppermute(moved, ("z", "y"), [(i, i + step) for i in range(0, halves, 2 * step)])
                moved = jnp.where(half % (2 * step) == step, got, moved)
                step //= 2
                stage += 1
                moved, bands = after(moved, bands, stage, stages)
            return padded(spread(moved)), unstage(band, bands), describe(ids, n0, blocks)

        return run

    def fetch_all(moved, band, rows, ids, n0):
        bands = stage_bands(band, rows)
        step = planes // 2
        while step:
            got = lax.ppermute(moved, "z", [(i, i + step) for i in range(0, planes, 2 * step)])
            moved = jnp.where(z % (2 * step) == step, got, moved)
            step //= 2
        across = lax.ppermute(moved, "y", [(0, 1), (1, 0)])
        moved = jnp.concatenate([jnp.where(y == 0, moved, across), jnp.where(y == 0, across, moved)])
        return tuple(spread(moved)), unstage(band, bands), describe(ids, n0, WIDE)

    prompt_set, (first_bands, other), (info, kinfo, rinfo) = lax.switch(
        level, [fetch(1), fetch(2), fetch_all], in_order, kv_both[0], rows_send, ids, n0
    )
    bands = [first_bands]

    for a in kv_both[1:]:
        a, _, prompt_set = lax.optimization_barrier((a, bands[-1], prompt_set))
        bands.append(send_bands(a))

    outs = None
    owns, prompts, wide_parts = [], [], []
    for i in range(SPLIT):
        column = heads * i
        sets = [(0, b) for b in bands[i]] + [(column, prompt_set)]
        outs, grads = attention(
            i, info, kinfo, rinfo, (query_rows, out_grad), other, sets, outs, group, heads
        )
        if owns:
            (outs, grads), owns[-1] = lax.optimization_barrier(((outs, grads), owns[-1]))
        if i < SPLIT - 1:
            owns.append(return_bands(grads))
        prompts.append(tuple(grads[3]))
        wide_parts.append(tuple(grads[4]))

    joined = lambda parts, k: jnp.concatenate([p[k] for p in parts], axis=3)

    def tree(back, axes, length, beside):
        step, stage, stages = 1, 1, length.bit_length()
        while step < length:
            back, beside = after(back, beside, stage, stages)
            got = lax.ppermute(back.astype(BF16), axes, [(j + step, j) for j in range(0, length, 2 * step)])
            back = back + got.astype(F32)
            step *= 2
            stage += 1
        return back, beside

    def give_back(blocks):
        def run(parts, band, rows):
            beside = stage_return(band, rows)
            arrays = []
            for k in range(n_sub):
                a = joined(parts[0], k)
                arrays.append(a if blocks == 1 else jnp.concatenate([a, joined(parts[1], k)[:1]]))
            back, (moved, near, arrived) = tree(gather_back(arrays), ("z", "y"), halves, beside)
            own = [band[0][0]] + moved[2] + near
            if blocks == 1:
                back = jnp.where((jnp.arange(CORES) == c)[:, None, None, None], back, 0.0)
            else:
                back = jnp.where(c == 0, back, back[::-1])
            return jnp.where(half == 0, back, 0.0), own, arrived

        return run

    def give_all_back(parts, band, rows):
        beside = stage_return(band, rows)
        back = gather_back(
            [jnp.concatenate([joined(parts[0], k), joined(parts[1], k)]) for k in range(n_sub)]
        ).astype(BF16)
        keep = jnp.where(y == 0, back[:2], back[2:])
        leave = jnp.where(y == 0, back[2:], back[:2])
        back = keep.astype(F32) + lax.ppermute(leave, "y", [(0, 1), (1, 0)]).astype(F32)
        back, (moved, near, arrived) = tree(back, "z", planes, beside)
        own = [band[0][0]] + moved[2] + near
        back = jnp.where(c == 0, back, back[::-1])
        return jnp.where(z == 0, back, 0.0), own, arrived

    back, last_own, arrived = lax.switch(
        level,
        [give_back(1), give_back(2), give_all_back],
        (tuple(prompts), tuple(wide_parts)),
        grads[:3],
        outs[2],
    )
    owns.append(last_own)
    total = back + jnp.concatenate([sum(a.astype(F32) for a in arrays) for arrays in owns], axis=3)
    total = total.astype(BF16)

    got = swap_cores(total[1])
    low = jnp.where(c == 0, total[0], got)
    high = jnp.where(c == 0, got, total[0])

    def columns_back(t):
        return jnp.concatenate([low[t], high[t]], axis=1)

    def join(full, part):
        return lax.dynamic_update_slice(full, part, (0, (1 - c) * part.shape[1]))

    return join(outs[0], arrived[0]), join(outs[1], arrived[1]), columns_back(0), columns_back(1)


def solution(mesh):
    blk, uly = mesh.shape["blk"], mesh.shape["uly"]
    parts = Mesh(np.asarray(mesh.devices).reshape(blk // 4, 2, CORES, uly), ALL)
    rows = P(ALL, None)
    return jax.shard_map(
        per_device,
        mesh=parts,
        in_specs=(rows, rows, rows, rows, P(ALL)),
        out_specs=(rows, rows, rows, rows),
        check_vma=False,
    )
```
